32 devices in a mesh: dp: 8 (over z, x), tp: 4 (over y, core).
Axes of the slice: x: 2, y: 2, z: 4, core: 2. Of those that a mesh axis runs over, the one named last changes fastest.
Arguments:
- activations: bfloat16 [2048, 4096], P(('dp', 'tp')), may hold values from -700 to 700
- cotangent: bfloat16 [2048, 512], P('dp', 'tp'), may hold values from -6 to 6
- segment_ids: int32 [2048], P('dp'), may hold values from 0 to 31, never falling along the last dimension, each value on 1 to 128 neighbouring positions
- norm_gain: float32 [4096], replicated, may hold values from 0.5 to 1.5
- query_weight: bfloat16 [4096, 512], P(None, 'tp'), may hold values from -2 to 2
- key_value_weight: bfloat16 [4096, 512], P(None, 'tp'), may hold values from -1 to 1
Outputs:
- input_grad: bfloat16 [2048, 4096], P(('dp', 'tp'))
- query_grad: bfloat16 [4096, 512], P(None, 'tp')
- key_value_grad: bfloat16 [4096, 512], P(None, 'tp')
- gain_grad: float32 [4096], replicated
The draws below stay inside these ranges and needn't reach their ends.
Inputs may be any that keep to these rules, and one draw needn't show every extreme that they name: `segment_ids`: document numbers never fall along the tokens; a document has 1 to 128 tokens and may run on from one replica's rows into the next.
All inputs are finite; a program needn't handle non-finite values.
Results may differ from the reference program's by a relative error of at most 0.03.
Values may be sent and summed in bfloat16 or wider, within the bound.
A program may use at most 64 MiB of HBM per device.

```python
import math
import jax
import jax.numpy as jnp
import numpy as np
from jax import lax

D = 4096
HD = 128
TOK = 256
H = 4
KV = 2
ALLTOK = 2048
SEGS = 32
N_DP = 8


def base_keys(key):
    return jax.random.truncated_normal(jax.random.fold_in(key, 3), -4.0, 4.0, (D, KV, HD), jnp.float32)


def draw_query_weight(key, part):
    noise = jax.random.truncated_normal(jax.random.fold_in(key, 7), -4.0, 4.0, (D, H, HD), jnp.float32)
    weights = noise
    return jnp.clip(weights / math.sqrt(D), -2.0, 2.0).reshape(D, H * HD).astype(jnp.bfloat16)


def draw_key_value_weight(key, part):
    keys_part = base_keys(key)
    values_part = jax.random.truncated_normal(jax.random.fold_in(key, 5), -4.0, 4.0, (D, KV, HD), jnp.float32)
    return (jnp.stack([keys_part, values_part], axis=2) / math.sqrt(D)).reshape(D, KV * 2 * HD).astype(jnp.bfloat16)


def draw_activations(key, part):
    base = jax.random.truncated_normal(jax.random.fold_in(key, 11), -4.0, 4.0, (ALLTOK, D), jnp.float32)
    column_scale = jnp.exp(jax.random.uniform(jax.random.fold_in(key, 13), (1, D), jnp.float32, 0.0, math.log(10.0)))
    row_scale = jnp.exp(jax.random.uniform(jax.random.fold_in(key, 17), (ALLTOK, 1), jnp.float32, 0.0, math.log(10.0)))
    return (base * column_scale * row_scale).astype(jnp.bfloat16)


def shard_levels(rng, extent, split, low, largest):
    factor_of, own = 1.0, jax.random.fold_in(rng, 6)
    for axis_at, shards_of in split:
        steps = jnp.exp(jax.random.uniform(jax.random.fold_in(own, axis_at), (shards_of,), jnp.float32, low / len(split), largest / len(split)))
        factor_of = factor_of * jnp.repeat(steps, extent[axis_at] // shards_of).reshape([-1 if axis == axis_at else 1 for axis in range(len(extent))])
    return factor_of


def profile(number_of, total, most, skew):
    weights = [(1 << 20) // math.isqrt(grade ** skew) + 1 for grade in range(2, number_of + 1)]
    rest, holding = total - most - (number_of - 1), [1] * (number_of - 1)
    while rest > 0:
        candidates = [i for i in range(number_of - 1) if holding[i] < most]
        mass, remaining = sum([weights[i] for i in candidates]), rest
        for i in candidates:
            addition = min(most - holding[i], max(1, remaining * weights[i] // mass), rest)
            holding[i] = holding[i] + addition
            rest = rest - addition
    return np.array([most] + holding)


def ragged(key, number_of, total, most, skew):
    if number_of == 2:
        one = jax.random.randint(key, (), max(1, total - most), min(most, total - 1) + 1)
        return jnp.stack([one, total - one])
    lengths = jnp.asarray(profile(number_of, total, most, skew), jnp.int32)
    pairs = (number_of - 1) // 2
    source_of, taker = lengths[1:1 + 2 * pairs:2], lengths[2:2 + 2 * pairs:2]
    slack = jnp.minimum(source_of - 1, most - taker)
    moved = jax.random.randint(jax.random.fold_in(key, 1), (pairs,), 0, 1 << 20) % (slack + 1)
    lengths = lengths.at[1:1 + 2 * pairs:2].set(source_of - moved).at[2:2 + 2 * pairs:2].set(taker + moved)
    return lengths[jax.random.permutation(jax.random.fold_in(key, 2), number_of)]


def bell_draw(key, extent, deviation, most, pieces=(), kind=jnp.bfloat16):
    gain = shard_levels(key, extent, pieces, -0.22, 0.18) if pieces else 1.0
    result = jax.random.normal(key, extent, jnp.float32) * deviation * gain
    return jnp.minimum(jnp.maximum(result, -most), most).astype(kind)


def setup_inputs(seed: int = 0) -> dict:
    key_list = jax.random.split(jax.random.key(seed), 7)
    return {
        "activations": draw_activations(jax.random.fold_in(key_list[6], 71), 0),
        "cotangent": bell_draw(key_list[1], (ALLTOK, H * HD), 1.0, 6.0, ((0, 8), (1, 4))),
        "segment_ids": jnp.searchsorted(jnp.cumsum(ragged(key_list[2], SEGS, ALLTOK, TOK // 2, 1)), jnp.arange(ALLTOK), side="right").astype(jnp.int32),
        "norm_gain": jnp.clip(1.0 + 0.1 * jax.random.normal(key_list[3], (D,), jnp.float32), 0.5, 1.5),
        "query_weight": draw_query_weight(jax.random.fold_in(key_list[6], 71), 0),
        "key_value_weight": draw_key_value_weight(jax.random.fold_in(key_list[6], 71), 0),
    }


EPS = 1e-05

def rope_tables():
    position = jnp.arange(TOK, dtype=jnp.float32)
    frequency = 500000.0 ** (-jnp.arange(0, HD, 2, dtype=jnp.float32) / HD)
    angle = position[:, None] * frequency[None, :]
    return (jnp.cos(angle)[:, None, :], jnp.sin(angle)[:, None, :])

def rotate(values, cosine, sine):
    half = HD // 2
    first = values[..., :half]
    second = values[..., half:]
    return jnp.concatenate([first * cosine - second * sine, second * cosine + first * sine], axis=-1)

def replica(activations, cotangent, segment_ids, norm_gain, query_weight, key_value_weight):
    inputs_f = activations.astype(jnp.float32)
    root_mean = jnp.sqrt(lax.optimization_barrier(jnp.mean(inputs_f * inputs_f, axis=1, keepdims=True)) + EPS)
    unit_rows = inputs_f / root_mean
    normed = (unit_rows * norm_gain[None, :]).astype(jnp.bfloat16)
    cosine, sine = rope_tables()
    query_raw = jnp.dot(normed, query_weight, preferred_element_type=jnp.float32).reshape(TOK, H, HD)
    pair_raw = jnp.dot(normed, key_value_weight, preferred_element_type=jnp.float32).reshape(TOK, KV, 2, HD)
    query = rotate(query_raw, cosine, sine).astype(jnp.bfloat16)
    keys = rotate(pair_raw[:, :, 0], cosine, sine).astype(jnp.bfloat16)
    values = pair_raw[:, :, 1].astype(jnp.bfloat16)
    keys_heads = jnp.repeat(keys, 2, axis=1).astype(jnp.float32)
    values_heads = jnp.repeat(values, 2, axis=1).astype(jnp.float32)
    query_f = query.astype(jnp.float32)
    scale = HD ** (-0.5)
    position = jnp.arange(TOK)
    allowed = (position[:, None] >= position[None, :]) & (segment_ids[:, None] == segment_ids[None, :])
    scores = jnp.einsum('thd,shd->hts', query_f, keys_heads) * scale
    scores = jnp.where(allowed[None], scores, jnp.float32(-1e+30))
    top = lax.optimization_barrier(jnp.max(scores, axis=2, keepdims=True))
    exp_scores = jnp.exp(scores - top)
    probs = exp_scores / lax.optimization_barrier(jnp.sum(exp_scores, axis=2, keepdims=True))
    probs_half = probs.astype(jnp.bfloat16)
    cot_heads = cotangent.reshape(TOK, H, HD).astype(jnp.float32)
    prob_grad = jnp.einsum('thd,shd->hts', cot_heads, values_heads)
    delta = lax.optimization_barrier(jnp.sum(probs * prob_grad, axis=2, keepdims=True))
    score_grad = (probs * (prob_grad - delta) * scale).astype(jnp.bfloat16).astype(jnp.float32)
    query_back = jnp.einsum('hts,shd->thd', score_grad, keys_heads)
    keys_back = jnp.einsum('hts,thd->shd', score_grad, query_f)
    values_back = jnp.einsum('hts,thd->shd', probs_half.astype(jnp.float32), cot_heads)
    query_part = rotate(query_back, cosine, -sine).astype(jnp.bfloat16)
    key_part = rotate(keys_back, cosine, -sine).astype(jnp.bfloat16)
    value_part = values_back.astype(jnp.bfloat16)
    query_flat = query_part.reshape(TOK, H * HD)
    key_sum = key_part.astype(jnp.float32).reshape(TOK, KV, 2, HD).sum(axis=2)
    value_sum = value_part.astype(jnp.float32).reshape(TOK, KV, 2, HD).sum(axis=2)
    pair_grad = jnp.stack([key_sum, value_sum], axis=2).reshape(TOK, KV * 2 * HD)
    query_term = jnp.dot(normed.T, query_flat, preferred_element_type=jnp.float32).astype(jnp.bfloat16)
    pair_term = jnp.dot(normed.astype(jnp.float32).T, pair_grad, precision=lax.Precision.HIGHEST).astype(jnp.bfloat16)
    normed_grad = jnp.dot(query_flat, query_weight.T, preferred_element_type=jnp.float32)
    normed_grad = normed_grad + jnp.dot(pair_grad, key_value_weight.astype(jnp.float32).T, precision=lax.Precision.HIGHEST)
    gain_term = lax.optimization_barrier(jnp.sum(normed_grad * unit_rows, axis=0))
    scaled = normed_grad * norm_gain[None, :]
    inner = lax.optimization_barrier(jnp.mean(scaled * unit_rows, axis=1, keepdims=True))
    input_grad = ((scaled - unit_rows * inner) / root_mean).astype(jnp.bfloat16)
    return (input_grad, query_term, pair_term, gain_term)

def reference(activations, cotangent, segment_ids, norm_gain, query_weight, key_value_weight):
    acts = activations.reshape(N_DP, TOK, D)
    cots = cotangent.reshape(N_DP, TOK, H * HD)
    segs = segment_ids.reshape(N_DP, TOK)

    def step(carry, inputs):
        input_grad, query_term, pair_term, gain_term = replica(inputs[0], inputs[1], inputs[2], norm_gain, query_weight, key_value_weight)
        query_sum, pair_sum, gain_sum = carry
        carry = (query_sum + query_term.astype(jnp.float32), pair_sum + pair_term.astype(jnp.float32), gain_sum + gain_term)
        return (carry, input_grad)
    start = (jnp.zeros((D, H * HD), jnp.float32), jnp.zeros((D, KV * 2 * HD), jnp.float32), jnp.zeros((D,), jnp.float32))
    (query_sum, pair_sum, gain_sum), grads = lax.scan(step, start, (acts, cots, segs))
    return (grads.reshape(N_DP * TOK, D), query_sum.astype(jnp.bfloat16), pair_sum.astype(jnp.bfloat16), gain_sum)
```

```python
import functools

import jax
import jax.numpy as jnp
import numpy as np
from jax import lax
from jax.experimental import pallas as pl
from jax.experimental.pallas import tpu as pltpu
from jax.sharding import PartitionSpec as P

EPS = 1e-05
AG_CHUNKS = 4
DP_CHUNKS = 16
LAGS = (0, 3, 6)
TASK_AT = 8
RS_CHUNKS = 4


def low_bit(d):
    return d & -d


def bits_of(n):
    return [1 << k for k in range(n.bit_length() - 1)]


def bit_at(v, b):
    return lax.rem(lax.div(v, b), 2)


def xor(v, mask):
    out = v
    for b in bits_of(1 << mask.bit_length()):
        if mask & b:
            out = out + b - 2 * b * bit_at(v, b)
    return out


def dot(a, b, ca, cb):
    return lax.dot_general(a, b, (((ca,), (cb,)), ((), ())), preferred_element_type=jnp.float32)


def kernel(ntp, ndp, x_hbm, cot_hbm, seg_hbm, gain_hbm, cos_hbm, sin_hbm, wq_ref, wkv_ref,
           ig_ref, qg_ref, kvg_ref, gg_ref,
           wcat, normed, normed_x, grads, grads_x, tot, rs_out, rs_in, term, chain, whole, gs, gr,
           kv_out, kv_in, inv_ref,
           w_sem, o_sem, ag_s, ag_r, nx_s, nx_r, gx_s, gx_r, rs_s, rs_r, in_s, in_r, down_s, down_r,
           last_s, last_r, g_s, g_r, kv_s, kv_r,
           x_ref, cot_ref, seg_ref, gain_ref, cos_ref, sin_ref, load_sem):
    tp, dp = lax.axis_index("tp"), lax.axis_index("dp")
    tp_bits, dp_bits = bits_of(ntp), bits_of(ndp)
    rows, width = x_ref.shape
    length = cot_ref.shape[0]
    head = cot_ref.shape[1]
    sends = []
    x, z, deep = lax.rem(dp, 2), lax.div(dp, 2), ndp // 2
    middle = deep // 2 - 1
    side = lax.div(z, deep // 2)
    depth = z + side * (deep - 1 - 2 * z)
    inner_dp = dp + 2 * (1 - 2 * side)
    outer_dp = dp - 2 * (1 - 2 * side)
    is_middle = lax.div(depth, middle) if middle else 1

    def to(src, dst, s, r, axis, device):
        return pltpu.make_async_remote_copy(
            src_ref=src, dst_ref=dst, send_sem=s, recv_sem=r,
            device_id={axis: device}, device_id_type=pl.DeviceIdType.MESH)

    def remote(src, dst, s, r, axis, b):
        return to(src, dst, s, r, axis, xor(tp if axis == "tp" else dp, b))

    def go(copy):
        copy.start()
        sends.append(copy)

    loads = [pltpu.make_async_copy(src, dst, load_sem.at[i]) for i, (src, dst) in enumerate((
        (x_hbm, x_ref), (gain_hbm, gain_ref), (cot_hbm, cot_ref), (seg_hbm, seg_ref),
        (cos_hbm, cos_ref), (sin_hbm, sin_ref)))]
    for copy in loads:
        copy.start()
    barrier = pltpu.get_barrier_semaphore()
    for b in tp_bits:
        pl.semaphore_signal(barrier, inc=1, device_id={"tp": xor(tp, b)},
                            device_id_type=pl.DeviceIdType.MESH)
    for b in dp_bits:
        pl.semaphore_signal(barrier, inc=1, device_id={"dp": xor(dp, b)},
                            device_id_type=pl.DeviceIdType.MESH)

    for step in (2, ndp - 2):
        pl.semaphore_signal(barrier, inc=1, device_id={"dp": lax.rem(dp + step, ndp)},
                            device_id_type=pl.DeviceIdType.MESH)

    w_copies = [pltpu.make_async_copy(wq_ref, wcat.at[:, 0:head], w_sem.at[0]),
                pltpu.make_async_copy(wkv_ref, wcat.at[:, head:2 * head], w_sem.at[1])]
    for copy in w_copies:
        copy.start()

    def block(d):
        return pl.ds(pl.multiple_of(xor(tp, d) * rows, rows), rows)

    cw = width // AG_CHUNKS

    def cols(c, w=cw):
        return slice(c * w, (c + 1) * w)

    for copy in loads:
        copy.wait()
    square = jnp.zeros((rows, 1), jnp.float32)
    for c in range(AG_CHUNKS):
        v = x_ref[:, cols(c)].astype(jnp.float32)
        square = square + jnp.sum(v * v, axis=1, keepdims=True)
    inv = 1.0 / jnp.sqrt(square * (1.0 / width) + EPS)
    inv_ref[...] = jnp.broadcast_to(inv, inv_ref.shape)

    half = width // 2
    held = AG_CHUNKS // 2

    def turn(c):
        at = lax.rem(c + held * (1 - x), AG_CHUNKS) * cw
        return pl.ds(pl.multiple_of(at, cw), cw)

    def nx(c, d):
        if d & 1:
            part = normed_x.at[block(d ^ 1), cols(c)]
            return remote(part, part, nx_s.at[c, d], nx_r.at[c, d], "tp", 1)
        return remote(normed.at[block(d), turn(c)], normed_x.at[block(d), cols(c)],
                      nx_s.at[c, d], nx_r.at[c, d], "dp", 1)

    def ag(c, d):
        b = low_bit(d)
        part = normed.at[block(d ^ b), turn(c)]
        return remote(part, part, ag_s.at[c, d], ag_r.at[c, d], "tp", b)

    order = sorted(range(1, ntp), key=lambda d: -low_bit(d))
    for c in range(AG_CHUNKS):
        unit = x_ref[:, turn(c)].astype(jnp.float32) * inv
        normed[block(0), turn(c)] = (unit * gain_ref[:, turn(c)]).astype(jnp.bfloat16)
        if c == 0:
            pl.semaphore_wait(barrier, len(tp_bits) + len(dp_bits) + 2)
        for b in reversed(tp_bits):
            go(ag(c, b))
        if c < held:
            go(nx(c, 0))
    for copy in w_copies:
        copy.wait()
    proj = jnp.zeros((length, 2 * head), jnp.float32)

    def forward(c):
        for d in order:
            if low_bit(d) > 1:
                ag(c, d).wait_recv()
                for b in reversed(tp_bits):
                    if b < low_bit(d):
                        go(ag(c, d | b))
                if c < held:
                    go(nx(c, d))

    def arrive(c, proj):
        for d in order:
            if low_bit(d) == 1:
                ag(c, d).wait_recv()
        return proj + dot(normed[:, turn(c)], wcat[turn(c), :], 1, 0)

    forward(0)
    for c in range(AG_CHUNKS):
        if c + 1 < AG_CHUNKS:
            forward(c + 1)
        if c == AG_CHUNKS - 1:
            for i in range(held):
                for d in range(0, ntp, 2):
                    nx(i, d).wait_recv()
                    go(nx(i, d | 1))
        proj = arrive(c, proj)

    odd = lax.rem(tp, 2) == 1
    cosine, sine = cos_ref[...], sin_ref[...]

    def rope(u):
        return u * cosine + pltpu.roll(u, head // 2, 1) * sine

    def rope_t(u):
        return u * cosine - pltpu.roll(u, head // 2, 1) * sine

    raw = proj[:, head:]
    own = jnp.where(odd, raw, rope(raw))
    kv_out[0] = own.astype(jnp.bfloat16)
    swap = remote(kv_out.at[0], kv_in.at[0], kv_s.at[0], kv_r.at[0], "tp", 1)
    go(swap)
    query = rope(proj[:, :head]).astype(jnp.bfloat16)
    seg_s = jnp.broadcast_to(seg_ref[...].astype(jnp.float32), (length, length))
    seg_t = seg_s.T
    t_at = lax.broadcasted_iota(jnp.int32, (length, length), 0)
    s_at = lax.broadcasted_iota(jnp.int32, (length, length), 1)
    allowed = (t_at >= s_at) & (seg_s == seg_t)
    scale = head ** (-0.5)
    swap.wait_recv()
    mine, other = kv_out[0].astype(jnp.float32), kv_in[0].astype(jnp.float32)
    keys = jnp.where(odd, other, mine).astype(jnp.bfloat16)
    values = jnp.where(odd, mine, other).astype(jnp.bfloat16)
    cot = cot_ref[...]
    scores = jnp.where(allowed, dot(query, keys, 1, 1) * scale, jnp.float32(-1e30))
    top = jnp.max(scores, axis=1, keepdims=True)
    e = jnp.exp(scores - top)
    probs = e / jnp.sum(e, axis=1, keepdims=True)
    prob_grad = dot(cot, values, 1, 1)
    delta = jnp.sum(probs * prob_grad, axis=1, keepdims=True)
    score_grad = (probs * (prob_grad - delta) * scale).astype(jnp.bfloat16)
    key_part = rope_t(dot(score_grad, query, 0, 0))
    value_part = dot(probs.astype(jnp.bfloat16), cot, 0, 0)
    kv_out[1] = jnp.where(odd, key_part, value_part).astype(jnp.bfloat16)
    swap = remote(kv_out.at[1], kv_in.at[1], kv_s.at[1], kv_r.at[1], "tp", 1)
    go(swap)
    own_grad = jnp.where(odd, value_part, key_part).astype(jnp.bfloat16).astype(jnp.float32)
    grads[:, :head] = rope_t(dot(score_grad, keys, 1, 0)).astype(jnp.bfloat16)
    swap.wait_recv()
    grads[:, head:] = (own_grad + kv_in[1].astype(jnp.float32)).astype(jnp.bfloat16)

    send_grads = remote(grads, grads_x, gx_s, gx_r, "dp", 1)
    go(send_grads)

    local = []
    size = half // DP_CHUNKS

    def mine_rows(q):
        return pl.ds(pl.multiple_of(x * half + q * size, size), size)

    def other_rows(q):
        return pl.ds(pl.multiple_of((1 - x) * half + q * size, size), size)

    def inward(q):
        return to(term.at[cols(q, size), :], chain.at[q, is_middle], in_s.at[q], in_r.at[q, is_middle],
                  "dp", inner_dp)

    def arrived(q, slot):
        return to(term.at[cols(q, size), :], chain.at[q, slot], in_s.at[q], in_r.at[q, slot], "dp", inner_dp)

    def outward(q):
        part = whole.at[mine_rows(q), :]
        return to(part, part, down_s.at[q], down_r.at[q], "dp", outer_dp)

    def final(q):
        part = whole.at[mine_rows(q), :]
        return remote(part, part, last_s.at[q], last_r.at[q], "dp", 1)

    def save(q, upper):
        for i, out in enumerate((qg_ref, kvg_ref)):
            at = other_rows(q) if upper else mine_rows(q)
            copy = pltpu.make_async_copy(
                whole.at[at, i * head:(i + 1) * head], out.at[at, :], o_sem.at[q, 2 * upper + i])
            copy.start()
            local.append(copy)

    def form(q):
        own = dot(normed[:, mine_rows(q)], grads[...], 0, 0)
        value = own + dot(normed_x[:, cols(q, size)], grads_x[...], 0, 0)
        term[cols(q, size), :] = value.astype(jnp.bfloat16)

        @pl.when(depth == 0)
        def _():
            inward(q).start()

    def gather(q):
        @pl.when(depth > 0)
        def _():
            arrived(q, 0).wait_recv()
            term[cols(q, size), :] = (term[cols(q, size), :].astype(jnp.float32)
                                      + chain[q, 0].astype(jnp.float32)).astype(jnp.bfloat16)
            inward(q).start()

    def finish(q):
        @pl.when(depth == middle)
        def _():
            arrived(q, 1).wait_recv()
            whole[mine_rows(q), :] = (term[cols(q, size), :].astype(jnp.float32)
                                      + chain[q, 1].astype(jnp.float32)).astype(jnp.bfloat16)

        @pl.when(depth < middle)
        def _():
            outward(q).wait_recv()

        @pl.when(depth > 0)
        def _():
            outward(q).start()

        go(final(q))
        save(q, 0)

    def end(q):
        final(q).wait_recv()
        save(q, 1)

    rw = width // RS_CHUNKS
    rs_order = sorted(range(1, ntp), key=low_bit)

    def rs(c, d):
        return remote(rs_out.at[d, :, cols(c, rw)], rs_in.at[d, :, cols(c, rw)],
                      rs_s.at[c, d], rs_r.at[c, d], "tp", low_bit(d))

    def partial(c, d):
        value = tot[block(d), cols(c, rw)]
        for b in tp_bits:
            if d == 0 or b < low_bit(d):
                value = value + rs_in[d | b, :, cols(c, rw)].astype(jnp.float32)
        return value

    def rs_send(c, b):
        for d in rs_order:
            if low_bit(d) == b:
                rs_out[d, :, cols(c, rw)] = partial(c, d).astype(jnp.bfloat16)
                go(rs(c, d))

    def rs_wait(c, b):
        for d in rs_order:
            if low_bit(d) == b:
                rs(c, d).wait_recv()

    def tp_task():
        for c in range(RS_CHUNKS):
            tot[:, cols(c, rw)] = dot(grads[...], wcat[cols(c, rw), :], 1, 1)
            rs_send(c, 1)
        yield
        for b in tp_bits[1:]:
            for c in range(RS_CHUNKS):
                rs_wait(c, b // 2)
                rs_send(c, b)
        yield
        inner = jnp.zeros((rows, 1), jnp.float32)
        scale_back = inv_ref[:, 0:1]
        for c in range(RS_CHUNKS):
            rs_wait(c, tp_bits[-1])
            value = partial(c, 0)
            tot[block(0), cols(c, rw)] = value
            product = value * (x_ref[:, cols(c, rw)].astype(jnp.float32) * scale_back)
            gs[0, :, cols(c, rw)] = jnp.sum(product, axis=0, keepdims=True)
            inner = inner + jnp.sum(product * gain_ref[:, cols(c, rw)], axis=1, keepdims=True)
        rounds = [("tp", b) for b in tp_bits] + [("dp", b) for b in dp_bits]

        def exchange(k):
            axis, b = rounds[k]
            return remote(gs.at[k], gr.at[k], g_s.at[k], g_r.at[k], axis, b)

        go(exchange(0))
        inner = inner * (1.0 / width)
        for c in range(RS_CHUNKS):
            unit = x_ref[:, cols(c, rw)].astype(jnp.float32) * scale_back
            scaled = tot[block(0), cols(c, rw)] * gain_ref[:, cols(c, rw)]
            ig_ref[:, cols(c, rw)] = ((scaled - unit * inner) * scale_back).astype(jnp.bfloat16)
        for k in range(len(rounds)):
            yield
            exchange(k).wait_recv()
            if k + 1 < len(rounds):
                gs[k + 1] = gs[k] + gr[k]
                go(exchange(k + 1))
            else:
                gg_ref[...] = gs[k] + gr[k]

    task = tp_task()
    next(task)
    send_grads.wait_recv()
    for i in range(held):
        for d in range(0, ntp, 2):
            nx(i, d | 1).wait_recv()
    for q in range(DP_CHUNKS // 2):
        form(q)
    next(task)
    for q in range(DP_CHUNKS // 2, DP_CHUNKS):
        form(q)
    for step in range(DP_CHUNKS + LAGS[2]):
        for lag, stage in zip(LAGS, (gather, finish, end)):
            if 0 <= step - lag < DP_CHUNKS:
                stage(step - lag)
        if step >= TASK_AT and (step - TASK_AT) % 2 == 0:
            next(task, None)
    for _ in task:
        pass
    for copy in local:
        copy.wait()
    for copy in sends:
        copy.wait_send()
    for q in range(DP_CHUNKS):
        inward(q).wait_send()

    @pl.when(depth > 0)
    def _():
        for q in range(DP_CHUNKS):
            outward(q).wait_send()


def store(*refs):
    copies = [pltpu.make_async_copy(refs[i], refs[4 + i], refs[8].at[i]) for i in range(4)]
    for copy in copies:
        copy.start()
    for copy in copies:
        copy.wait()


def on_device(ntp, ndp, activations, cotangent, segment_ids, norm_gain, query_weight, key_value_weight):
    rows, width = activations.shape
    length, head = cotangent.shape
    angle = np.arange(length)[:, None] * 500000.0 ** (-np.arange(0, head, 2) / head)[None, :]
    cosine = np.concatenate([np.cos(angle), np.cos(angle)], axis=1).astype(np.float32)
    sine = np.concatenate([-np.sin(angle), np.sin(angle)], axis=1).astype(np.float32)
    nb = len(bits_of(ntp)) + len(bits_of(ndp))
    bf, f32 = jnp.bfloat16, jnp.float32
    vmem = pl.BlockSpec(memory_space=pltpu.VMEM)
    anywhere = pl.BlockSpec(memory_space=pl.ANY)
    hbm = pl.BlockSpec(memory_space=pltpu.HBM)
    dma = pltpu.SemaphoreType.DMA
    outs = pl.pallas_call(
        functools.partial(kernel, ntp, ndp),
        out_shape=[
            pltpu.VMEM((rows, width), bf),
            pltpu.VMEM((width, head), bf),
            pltpu.VMEM((width, head), bf),
            pltpu.VMEM((1, width), f32),
        ],
        in_specs=[hbm] * 8,
        out_specs=[vmem, vmem, vmem, vmem],
        scratch_shapes=[
            pltpu.VMEM((width, 2 * head), bf),
            pltpu.VMEM((length, width), bf),
            pltpu.VMEM((length, width // 2), bf),
            pltpu.VMEM((length, 2 * head), bf),
            pltpu.VMEM((length, 2 * head), bf),
            pltpu.VMEM((length, width), f32),
            pltpu.VMEM((ntp, rows, width), bf),
            pltpu.VMEM((ntp, rows, width), bf),
            pltpu.VMEM((width // 2, 2 * head), bf),
            pltpu.VMEM((DP_CHUNKS, 2, width // 2 // DP_CHUNKS, 2 * head), bf),
            pltpu.VMEM((width, 2 * head), bf),
            pltpu.VMEM((nb, 1, width), f32),
            pltpu.VMEM((nb, 1, width), f32),
            pltpu.VMEM((2, length, head), bf),
            pltpu.VMEM((2, length, head), bf),
            pltpu.VMEM((rows, 128), f32),
            dma((2,)),
            dma((DP_CHUNKS, 4)),
            dma((AG_CHUNKS, ntp)),
            dma((AG_CHUNKS, ntp)),
            dma((AG_CHUNKS // 2, ntp)),
            dma((AG_CHUNKS // 2, ntp)),
            dma,
            dma,
            dma((RS_CHUNKS, ntp)),
            dma((RS_CHUNKS, ntp)),
            dma((DP_CHUNKS,)),
            dma((DP_CHUNKS, 2)),
            dma((DP_CHUNKS,)),
            dma((DP_CHUNKS,)),
            dma((DP_CHUNKS,)),
            dma((DP_CHUNKS,)),
            dma((nb,)),
            dma((nb,)),
            dma((2,)),
            dma((2,)),
            pltpu.VMEM((rows, width), bf),
            pltpu.VMEM((length, head), bf),
            pltpu.VMEM((1, length), jnp.int32),
            pltpu.VMEM((1, width), f32),
            pltpu.VMEM((length, head), f32),
            pltpu.VMEM((length, head), f32),
            dma((6,)),
        ],
        compiler_params=pltpu.CompilerParams(
            collective_id=0, has_side_effects=True, vmem_limit_bytes=40 * 1024 * 1024),
    )(*[pltpu.with_memory_space_constraint(v, pltpu.HBM) for v in (
        activations, cotangent, segment_ids.reshape(1, length), norm_gain.reshape(1, width),
        jnp.asarray(cosine), jnp.asarray(sine), query_weight, key_value_weight)])
    outs = pl.pallas_call(
        store,
        out_shape=[
            jax.ShapeDtypeStruct((rows, width), bf),
            jax.ShapeDtypeStruct((width, head), bf),
            jax.ShapeDtypeStruct((width, head), bf),
            jax.ShapeDtypeStruct((1, width), f32),
        ],
        in_specs=[vmem] * 4,
        out_specs=[hbm] * 4,
        scratch_shapes=[dma((4,))],
    )(*[pltpu.with_memory_space_constraint(v, pltpu.VMEM) for v in outs])
    return (outs[0], outs[1], outs[2], outs[3].reshape(width))


def solution(mesh):
    return jax.shard_map(
        functools.partial(on_device, mesh.shape["tp"], mesh.shape["dp"]),
        mesh=mesh,
        in_specs=(P(("dp", "tp"), None), P("dp", "tp"), P("dp"), P(), P(None, "tp"), P(None, "tp")),
        out_specs=(P(("dp", "tp"), None), P(None, "tp"), P(None, "tp"), P()),
        check_vma=False,
    )
```

```python
import functools

import jax
import jax.numpy as jnp
import numpy as np
from jax import lax
from jax.experimental import pallas as pl
from jax.experimental.pallas import tpu as pltpu
from jax.sharding import PartitionSpec as P

EPS = 1e-05
AG_CHUNKS = 4
BLOCK = 128
OUTER_LAG, MIDDLE_LAG = 10, 4
RS_CHUNKS = 8
FIRST_BACK, FORM_AT, FORMS, REST_AT, LAST_AT, GAIN_EVERY, GAIN_AT = 3, 4, 3, 5, 14, 5, 28


def low_bit(d):
    return d & -d


def bits_of(n):
    return [1 << k for k in range(n.bit_length() - 1)]


def bit_at(v, b):
    return lax.rem(lax.div(v, b), 2)


def xor(v, mask):
    out = v
    for b in bits_of(1 << mask.bit_length()):
        if mask & b:
            out = out + b - 2 * b * bit_at(v, b)
    return out


def dot(a, b, ca, cb):
    return lax.dot_general(a, b, (((ca,), (cb,)), ((), ())), preferred_element_type=jnp.float32)


def kernel(ntp, ndp, x_hbm, cot_hbm, seg_hbm, gain_hbm, cos_hbm, sin_hbm, wq_ref, wkv_ref,
           ig_ref, qg_ref, kvg_ref, gg_ref,
           wcat, normed, normed_x, grads, grads_x, tot, rs_out, rs_in, term, chain, weigh, gs, gr, gsum, gchain,
           kv_out, kv_in, inv_ref,
           w_sem, ag_s, ag_r, nx_s, nx_r, gx_s, gx_r, rs_s, rs_r, in_s, in_r, down_s, down_r,
           last_s, last_r, g_s, g_r, kv_s, kv_r,
           x_ref, cot_ref, seg_ref, gain_ref, cos_ref, sin_ref, load_sem):
    tp, dp = lax.axis_index("tp"), lax.axis_index("dp")
    tp_bits, dp_bits = bits_of(ntp), bits_of(ndp)
    rows, width = x_ref.shape
    length = cot_ref.shape[0]
    head = cot_ref.shape[1]
    sends = []
    x, z, deep = lax.rem(dp, 2), lax.div(dp, 2), ndp // 2
    middle = deep // 2 - 1
    side = lax.div(z, deep // 2)
    depth = z + side * (deep - 1 - 2 * z)
    inner_dp = dp + 2 * (1 - 2 * side)
    outer_dp = dp - 2 * (1 - 2 * side)
    is_middle = lax.div(depth, middle) if middle else 1

    def to(src, dst, s, r, axis, device):
        return pltpu.make_async_remote_copy(
            src_ref=src, dst_ref=dst, send_sem=s, recv_sem=r,
            device_id={axis: device}, device_id_type=pl.DeviceIdType.MESH)

    def remote(src, dst, s, r, axis, b):
        return to(src, dst, s, r, axis, xor(tp if axis == "tp" else dp, b))

    def go(copy):
        copy.start()
        sends.append(copy)

    loads = [pltpu.make_async_copy(src, dst, load_sem.at[i]) for i, (src, dst) in enumerate((
        (x_hbm, x_ref), (gain_hbm, gain_ref), (cot_hbm, cot_ref), (seg_hbm, seg_ref),
        (cos_hbm, cos_ref), (sin_hbm, sin_ref)))]
    for copy in loads:
        copy.start()
    barrier = pltpu.get_barrier_semaphore()
    for b in tp_bits:
        pl.semaphore_signal(barrier, inc=1, device_id={"tp": xor(tp, b)},
                            device_id_type=pl.DeviceIdType.MESH)
    for b in dp_bits:
        pl.semaphore_signal(barrier, inc=1, device_id={"dp": xor(dp, b)},
                            device_id_type=pl.DeviceIdType.MESH)

    for step in (2, ndp - 2):
        pl.semaphore_signal(barrier, inc=1, device_id={"dp": lax.rem(dp + step, ndp)},
                            device_id_type=pl.DeviceIdType.MESH)

    w_copies = [pltpu.make_async_copy(wq_ref, wcat.at[:, 0:head], w_sem.at[0]),
                pltpu.make_async_copy(wkv_ref, wcat.at[:, head:2 * head], w_sem.at[1])]
    for copy in w_copies:
        copy.start()

    def block(d):
        return pl.ds(pl.multiple_of(xor(tp, d) * rows, rows), rows)

    cw = width // AG_CHUNKS

    def cols(c, w=cw):
        return slice(c * w, (c + 1) * w)

    for copy in loads[:2]:
        copy.wait()
    square = jnp.zeros((rows, 1), jnp.float32)
    for c in range(AG_CHUNKS):
        v = x_ref[:, cols(c)].astype(jnp.float32)
        square = square + jnp.sum(v * v, axis=1, keepdims=True)
    inv = 1.0 / jnp.sqrt(square * (1.0 / width) + EPS)
    inv_ref[...] = jnp.broadcast_to(inv, inv_ref.shape)

    half = width // 2
    held = AG_CHUNKS // 2

    def turn(c):
        at = lax.rem(c + held * (1 - x), AG_CHUNKS) * cw
        return pl.ds(pl.multiple_of(at, cw), cw)

    def nx(c, d):
        if d & 1:
            part = normed_x.at[block(d ^ 1), cols(c)]
            return remote(part, part, nx_s.at[c, d], nx_r.at[c, d], "tp", 1)
        return remote(normed.at[block(d), turn(c)], normed_x.at[block(d), cols(c)],
                      nx_s.at[c, d], nx_r.at[c, d], "dp", 1)

    def ag(c, d):
        b = low_bit(d)
        part = normed.at[block(d ^ b), turn(c)]
        return remote(part, part, ag_s.at[c, d], ag_r.at[c, d], "tp", b)

    order = sorted(range(1, ntp), key=lambda d: -low_bit(d))
    for c in range(AG_CHUNKS):
        unit = x_ref[:, turn(c)].astype(jnp.float32) * inv
        normed[block(0), turn(c)] = (unit * gain_ref[:, turn(c)]).astype(jnp.bfloat16)
        if c == 0:
            pl.semaphore_wait(barrier, len(tp_bits) + len(dp_bits) + 2)
        for b in reversed(tp_bits):
            go(ag(c, b))
        if c < held:
            go(nx(c, 0))
    for copy in w_copies + loads[2:]:
        copy.wait()
    proj = jnp.zeros((length, 2 * head), jnp.float32)

    def forward(c):
        for d in order:
            if low_bit(d) > 1:
                ag(c, d).wait_recv()
                for b in reversed(tp_bits):
                    if b < low_bit(d):
                        go(ag(c, d | b))
                if c < held:
                    go(nx(c, d))

    def arrive(c, proj):
        for d in order:
            if low_bit(d) == 1:
                ag(c, d).wait_recv()
        return proj + dot(normed[:, turn(c)], wcat[turn(c), :], 1, 0)

    def share(i):
        for d in range(0, ntp, 2):
            nx(i, d).wait_recv()
            go(nx(i, d | 1))

    forward(0)
    for c in range(AG_CHUNKS):
        if c + 1 < AG_CHUNKS:
            forward(c + 1)
        if c == AG_CHUNKS - 1:
            for i in range(held - 1):
                share(i)
        proj = arrive(c, proj)

    odd = lax.rem(tp, 2) == 1
    cosine, sine = cos_ref[...], sin_ref[...]

    def rope(u):
        return u * cosine + pltpu.roll(u, head // 2, 1) * sine

    def rope_t(u):
        return u * cosine - pltpu.roll(u, head // 2, 1) * sine

    raw = proj[:, head:]
    own = jnp.where(odd, raw, rope(raw))
    kv_out[0] = own.astype(jnp.bfloat16)
    swap = remote(kv_out.at[0], kv_in.at[0], kv_s.at[0], kv_r.at[0], "tp", 1)
    go(swap)
    share(held - 1)
    query = rope(proj[:, :head]).astype(jnp.bfloat16)
    seg_s = jnp.broadcast_to(seg_ref[...].astype(jnp.float32), (length, length))
    seg_t = seg_s.T
    t_at = lax.broadcasted_iota(jnp.int32, (length, length), 0)
    s_at = lax.broadcasted_iota(jnp.int32, (length, length), 1)
    allowed = (t_at >= s_at) & (seg_s == seg_t)
    scale = head ** (-0.5)
    swap.wait_recv()
    mine, other = kv_out[0].astype(jnp.float32), kv_in[0].astype(jnp.float32)
    keys = jnp.where(odd, other, mine).astype(jnp.bfloat16)
    values = jnp.where(odd, mine, other).astype(jnp.bfloat16)
    cot = cot_ref[...]
    scores = jnp.where(allowed, dot(query, keys, 1, 1) * scale, jnp.float32(-1e30))
    top = jnp.max(scores, axis=1, keepdims=True)
    e = jnp.exp(scores - top)
    probs = e / jnp.sum(e, axis=1, keepdims=True)
    prob_grad = dot(cot, values, 1, 1)
    delta = jnp.sum(probs * prob_grad, axis=1, keepdims=True)
    score_grad = (probs * (prob_grad - delta) * scale).astype(jnp.bfloat16)
    grads[:, :head] = rope_t(dot(score_grad, keys, 1, 0)).astype(jnp.bfloat16)

    def gx(p):
        at = slice(p * head, (p + 1) * head)
        return remote(grads.at[:, at], grads_x.at[:, at], gx_s.at[p], gx_r.at[p], "dp", 1)

    go(gx(0))
    key_part = rope_t(dot(score_grad, query, 0, 0))
    value_part = dot(probs.astype(jnp.bfloat16), cot, 0, 0)
    kv_out[1] = jnp.where(odd, key_part, value_part).astype(jnp.bfloat16)
    swap = remote(kv_out.at[1], kv_in.at[1], kv_s.at[1], kv_r.at[1], "tp", 1)
    go(swap)
    own_grad = jnp.where(odd, value_part, key_part).astype(jnp.bfloat16).astype(jnp.float32)
    swap.wait_recv()
    grads[:, head:] = (own_grad + kv_in[1].astype(jnp.float32)).astype(jnp.bfloat16)
    go(gx(1))

    blocks = half // BLOCK
    chunks = 2 * blocks
    whole = (qg_ref, kvg_ref)

    def local_rows(q):
        at = (q % blocks) * BLOCK
        return slice(at, at + BLOCK)

    def mine_rows(q):
        return pl.ds(pl.multiple_of(x * half + (q % blocks) * BLOCK, BLOCK), BLOCK)

    def mine(q):
        return term.at[q // blocks, local_rows(q), :]

    def inward(q):
        if q == chunks:
            return to(gsum, gchain.at[is_middle], in_s.at[q], in_r.at[q, is_middle], "dp", inner_dp)
        return to(mine(q), chain.at[q, is_middle], in_s.at[q], in_r.at[q, is_middle], "dp", inner_dp)

    def arrived(q, slot):
        if q == chunks:
            return to(gsum, gchain.at[slot], in_s.at[q], in_r.at[q, slot], "dp", inner_dp)
        return to(mine(q), chain.at[q, slot], in_s.at[q], in_r.at[q, slot], "dp", inner_dp)

    half_at = pl.ds(pl.multiple_of(x * half, half), half)

    def result_part(q):
        if q == chunks:
            return gg_ref.at[:, half_at]
        return whole[q // blocks].at[mine_rows(q), :]

    def outward(q):
        part = result_part(q)
        return to(part, part, down_s.at[q], down_r.at[q], "dp", outer_dp)

    def final(q):
        part = result_part(q)
        return remote(part, part, last_s.at[q], last_r.at[q], "dp", 1)

    def form(q):
        at = slice(q // blocks * head, (q // blocks + 1) * head)
        value = dot(normed[:, mine_rows(q)], grads[:, at], 0, 0)
        value = value + dot(normed_x[:, local_rows(q)], grads_x[:, at], 0, 0)
        term[q // blocks, local_rows(q), :] = value.astype(jnp.bfloat16)

        @pl.when(depth == 0)
        def _():
            inward(q).start()

        value = value * wcat[mine_rows(q), at].astype(jnp.float32)
        if q < blocks:
            weigh[local_rows(q), :] = value
        else:
            value = value + weigh[local_rows(q), :]
            gs[0, :, local_rows(q)] = jnp.sum(value.T, axis=0, keepdims=True)

    def plus(q, slot):
        value = term[q // blocks, local_rows(q), :].astype(jnp.float32)
        return (value + chain[q, slot].astype(jnp.float32)).astype(jnp.bfloat16)

    def gather(q):
        @pl.when(depth > 0)
        def _():
            arrived(q, 0).wait_recv()
            if q == chunks:
                gsum[...] = gsum[...] + gchain[0]
            else:
                term[q // blocks, local_rows(q), :] = plus(q, 0)
            inward(q).start()

    def turn_back(q):
        @pl.when(depth == middle)
        def _():
            arrived(q, 1).wait_recv()
            if q == chunks:
                gg_ref[:, half_at] = (gsum[...] + gchain[1]) / gain_ref[:, half_at]
            else:
                whole[q // blocks][mine_rows(q), :] = plus(q, 1)
            outward(q).start()
            final(q).start()

    def pass_on(q):
        @pl.when(depth < middle)
        def _():
            outward(q).wait_recv()

            @pl.when(depth > 0)
            def _():
                outward(q).start()

            final(q).start()

    rw = width // RS_CHUNKS
    rs_order = sorted(range(1, ntp), key=low_bit)

    def rs(c, d):
        return remote(rs_out.at[d, :, cols(c, rw)], rs_in.at[d, :, cols(c, rw)],
                      rs_s.at[c, d], rs_r.at[c, d], "tp", low_bit(d))

    def partial(c, d):
        value = tot[block(d), cols(c, rw)]
        for b in tp_bits:
            if d == 0 or b < low_bit(d):
                value = value + rs_in[d | b, :, cols(c, rw)].astype(jnp.float32)
        return value

    def rs_send(c, b):
        for d in rs_order:
            if low_bit(d) == b:
                rs_out[d, :, cols(c, rw)] = partial(c, d).astype(jnp.bfloat16)
                go(rs(c, d))

    def rs_wait(c, b):
        for d in rs_order:
            if low_bit(d) == b:
                rs(c, d).wait_recv()

    def back(c):
        tot[:, cols(c, rw)] = dot(grads[...], wcat[cols(c, rw), :], 1, 1)
        rs_send(c, 1)

    def rest(c, b):
        rs_wait(c, b // 2)
        rs_send(c, b)

    scale_back = inv_ref[:, 0:1]

    def exchange(k):
        return remote(gs.at[k], gr.at[k], g_s.at[k], g_r.at[k], "tp", tp_bits[k])

    def add_up(k):
        exchange(k).wait_recv()
        if k + 1 < len(tp_bits):
            gs[k + 1] = gs[k] + gr[k]
            go(exchange(k + 1))
        else:
            gsum[...] = gs[k] + gr[k]

            @pl.when(depth == 0)
            def _():
                inward(chunks).start()

    inner = [jnp.zeros((rows, 1), jnp.float32)]

    def unit(c):
        return x_ref[:, cols(c, rw)].astype(jnp.float32) * scale_back

    def project(c):
        rs_wait(c, tp_bits[-1])
        scaled = partial(c, 0) * gain_ref[:, cols(c, rw)]
        tot[block(0), cols(c, rw)] = scaled
        inner[0] = inner[0] + jnp.sum(scaled * unit(c), axis=1, keepdims=True)

    def result(c):
        scaled = tot[block(0), cols(c, rw)]
        ig_ref[:, cols(c, rw)] = ((scaled - unit(c) * (inner[0] * (1.0 / width))) * scale_back).astype(jnp.bfloat16)

    work = []

    def later(step, f, *args):
        work.append((step, len(work), functools.partial(f, *args)))

    for c in range(FIRST_BACK):
        back(c)
    for i in range(held):
        for d in range(0, ntp, 2):
            nx(i, d | 1).wait_recv()
    gx(0).wait_recv()
    for q in range(blocks):
        form(q)
    for c in range(FIRST_BACK, RS_CHUNKS):
        later(c - FIRST_BACK, back, c)
    later(FORM_AT, lambda: gx(1).wait_recv())
    for q in range(blocks, chunks):
        at = FORM_AT + (q - blocks) // FORMS
        later(at, form, q)
    later(at, lambda: go(exchange(0)))
    for k in range(len(tp_bits)):
        later(at + GAIN_EVERY * (k + 1), add_up, k)
    at = max(GAIN_AT, at + GAIN_EVERY * len(tp_bits) + 1)
    later(at, gather, chunks)
    later(at + MIDDLE_LAG, turn_back, chunks)
    later(at + OUTER_LAG, pass_on, chunks)
    for i, b in enumerate(tp_bits[1:]):
        for c in range(RS_CHUNKS):
            later(REST_AT + i * RS_CHUNKS + c, rest, c, b)
    at = LAST_AT + (len(tp_bits) - 2) * RS_CHUNKS
    for c in range(RS_CHUNKS):
        later(at + 2 * c, project, c)
    for c in range(RS_CHUNKS):
        later(at + 2 * RS_CHUNKS + c, result, c)
    work.sort(key=lambda w: w[:2])
    for step in range(chunks + max(OUTER_LAG, MIDDLE_LAG)):
        if step < chunks:
            gather(step)
        if 0 <= step - MIDDLE_LAG < chunks:
            turn_back(step - MIDDLE_LAG)
        if 0 <= step - OUTER_LAG < chunks:
            pass_on(step - OUTER_LAG)
        while work and work[0][0] <= step:
            work.pop(0)[2]()
    for _, _, f in work:
        f()
    for q in range(chunks + 1):
        final(q).wait_recv()
    for copy in sends:
        copy.wait_send()
    for q in range(chunks + 1):
        inward(q).wait_send()
        final(q).wait_send()

    @pl.when(depth > 0)
    def _():
        for q in range(chunks + 1):
            outward(q).wait_send()


def store(*refs):
    copies = [pltpu.make_async_copy(refs[i], refs[4 + i], refs[8].at[i]) for i in range(4)]
    for copy in copies:
        copy.start()
    for copy in copies:
        copy.wait()


def on_device(ntp, ndp, activations, cotangent, segment_ids, norm_gain, query_weight, key_value_weight):
    rows, width = activations.shape
    length, head = cotangent.shape
    angle = np.arange(length)[:, None] * 500000.0 ** (-np.arange(0, head, 2) / head)[None, :]
    cosine = np.concatenate([np.cos(angle), np.cos(angle)], axis=1).astype(np.float32)
    sine = np.concatenate([-np.sin(angle), np.sin(angle)], axis=1).astype(np.float32)
    chunks = width // BLOCK
    nb = len(bits_of(ntp))
    bf, f32 = jnp.bfloat16, jnp.float32
    vmem = pl.BlockSpec(memory_space=pltpu.VMEM)
    anywhere = pl.BlockSpec(memory_space=pl.ANY)
    hbm = pl.BlockSpec(memory_space=pltpu.HBM)
    dma = pltpu.SemaphoreType.DMA
    outs = pl.pallas_call(
        functools.partial(kernel, ntp, ndp),
        out_shape=[
            pltpu.VMEM((rows, width), bf),
            pltpu.VMEM((width, head), bf),
            pltpu.VMEM((width, head), bf),
            pltpu.VMEM((1, width), f32),
        ],
        in_specs=[hbm] * 8,
        out_specs=[vmem, vmem, vmem, vmem],
        scratch_shapes=[
            pltpu.VMEM((width, 2 * head), bf),
            pltpu.VMEM((length, width), bf),
            pltpu.VMEM((length, width // 2), bf),
            pltpu.VMEM((length, 2 * head), bf),
            pltpu.VMEM((length, 2 * head), bf),
            pltpu.VMEM((length, width), f32),
            pltpu.VMEM((ntp, rows, width), bf),
            pltpu.VMEM((ntp, rows, width), bf),
            pltpu.VMEM((2, width // 2, head), bf),
            pltpu.VMEM((chunks, 2, BLOCK, head), bf),
            pltpu.VMEM((width // 2, head), f32),
            pltpu.VMEM((nb, 1, width // 2), f32),
            pltpu.VMEM((nb, 1, width // 2), f32),
            pltpu.VMEM((1, width // 2), f32),
            pltpu.VMEM((2, 1, width // 2), f32),
            pltpu.VMEM((2, length, head), bf),
            pltpu.VMEM((2, length, head), bf),
            pltpu.VMEM((rows, 128), f32),
            dma((2,)),
            dma((AG_CHUNKS, ntp)),
            dma((AG_CHUNKS, ntp)),
            dma((AG_CHUNKS // 2, ntp)),
            dma((AG_CHUNKS // 2, ntp)),
            dma((2,)),
            dma((2,)),
            dma((RS_CHUNKS, ntp)),
            dma((RS_CHUNKS, ntp)),
            dma((chunks + 1,)),
            dma((chunks + 1, 2)),
            dma((chunks + 1,)),
            dma((chunks + 1,)),
            dma((chunks + 1,)),
            dma((chunks + 1,)),
            dma((nb,)),
            dma((nb,)),
            dma((2,)),
            dma((2,)),
            pltpu.VMEM((rows, width), bf),
            pltpu.VMEM((length, head), bf),
            pltpu.VMEM((1, length), jnp.int32),
            pltpu.VMEM((1, width), f32),
            pltpu.VMEM((length, head), f32),
            pltpu.VMEM((length, head), f32),
            dma((6,)),
        ],
        compiler_params=pltpu.CompilerParams(
            collective_id=0, has_side_effects=True, vmem_limit_bytes=40 * 1024 * 1024),
    )(*[pltpu.with_memory_space_constraint(v, pltpu.HBM) for v in (
        activations, cotangent, segment_ids.reshape(1, length), norm_gain.reshape(1, width),
        jnp.asarray(cosine), jnp.asarray(sine), query_weight, key_value_weight)])
    outs = pl.pallas_call(
        store,
        out_shape=[
            jax.ShapeDtypeStruct((rows, width), bf),
            jax.ShapeDtypeStruct((width, head), bf),
            jax.ShapeDtypeStruct((width, head), bf),
            jax.ShapeDtypeStruct((1, width), f32),
        ],
        in_specs=[vmem] * 4,
        out_specs=[hbm] * 4,
        scratch_shapes=[dma((4,))],
    )(*[pltpu.with_memory_space_constraint(v, pltpu.VMEM) for v in outs])
    return (outs[0], outs[1], outs[2], outs[3].reshape(width))


def solution(mesh):
    return jax.shard_map(
        functools.partial(on_device, mesh.shape["tp"], mesh.shape["dp"]),
        mesh=mesh,
        in_specs=(P(("dp", "tp"), None), P("dp", "tp"), P("dp"), P(), P(None, "tp"), P(None, "tp")),
        out_specs=(P(("dp", "tp"), None), P(None, "tp"), P(None, "tp"), P()),
        check_vma=False,
    )
```

```python
import functools

import jax
import jax.numpy as jnp
import numpy as np
from jax import lax
from jax.experimental import pallas as pl
from jax.experimental.pallas import tpu as pltpu
from jax.sharding import PartitionSpec as P

EPS = 1e-05
AG_CHUNKS = 4
BLOCK = 128
OUTER_LAG, MIDDLE_LAG = 10, 4
RS_CHUNKS = 8
FIRST_BACK, FORM_AT, FORMS, REST_AT, LAST_AT, GAIN_EVERY, GAIN_AT = 3, 4, 3, 5, 14, 5, 28


def low_bit(d):
    return d & -d


def bits_of(n):
    return [1 << k for k in range(n.bit_length() - 1)]


def bit_at(v, b):
    return lax.rem(lax.div(v, b), 2)


def xor(v, mask):
    out = v
    for b in bits_of(1 << mask.bit_length()):
        if mask & b:
            out = out + b - 2 * b * bit_at(v, b)
    return out


def dot(a, b, ca, cb):
    return lax.dot_general(a, b, (((ca,), (cb,)), ((), ())), preferred_element_type=jnp.float32)


def kernel(ntp, ndp, x_hbm, cot_hbm, seg_hbm, gain_hbm, rope_hbm, wq_ref, wkv_ref,
           ig_ref, qg_ref, kvg_ref, gg_ref,
           wcat, normed, normed_x, grads, grads_x, tot, rs_out, rs_in, term, chain, weigh, gs, gr, gsum, gchain,
           kv_out, kv_in, inv_ref,
           w_sem, ag_s, ag_r, nx_s, nx_r, gx_s, gx_r, rs_s, rs_r, in_s, chain_r, down_s,
           last_s, last_r, g_s, g_r, kv_s, kv_r,
           x_ref, cot_ref, seg_ref, gain_ref, rope_ref, load_sem):
    tp, dp = lax.axis_index("tp"), lax.axis_index("dp")
    tp_bits, dp_bits = bits_of(ntp), bits_of(ndp)
    rows, width = x_ref.shape
    length = cot_ref.shape[0]
    head = cot_ref.shape[1]
    x, z, deep = lax.rem(dp, 2), lax.div(dp, 2), ndp // 2
    middle = deep // 2 - 1
    side = lax.div(z, deep // 2)
    depth = z + side * (deep - 1 - 2 * z)
    inner_dp = dp + 2 * (1 - 2 * side)
    outer_dp = dp - 2 * (1 - 2 * side)
    is_middle = lax.div(depth, middle) if middle else 1

    def to(src, dst, s, r, axis, device):
        return pltpu.make_async_remote_copy(
            src_ref=src, dst_ref=dst, send_sem=s, recv_sem=r,
            device_id={axis: device}, device_id_type=pl.DeviceIdType.MESH)

    def remote(src, dst, s, r, axis, b):
        return to(src, dst, s, r, axis, xor(tp if axis == "tp" else dp, b))

    loads = [pltpu.make_async_copy(src, dst, load_sem.at[i]) for i, (src, dst) in enumerate((
        (x_hbm, x_ref), (gain_hbm, gain_ref), (cot_hbm, cot_ref), (seg_hbm, seg_ref),
        (rope_hbm, rope_ref)))]
    for copy in loads:
        copy.start()
    barrier = pltpu.get_barrier_semaphore()
    for b in tp_bits:
        pl.semaphore_signal(barrier, inc=1, device_id={"tp": xor(tp, b)},
                            device_id_type=pl.DeviceIdType.MESH)
    for b in dp_bits:
        pl.semaphore_signal(barrier, inc=1, device_id={"dp": xor(dp, b)},
                            device_id_type=pl.DeviceIdType.MESH)

    for step in (2, ndp - 2):
        pl.semaphore_signal(barrier, inc=1, device_id={"dp": lax.rem(dp + step, ndp)},
                            device_id_type=pl.DeviceIdType.MESH)

    w_copies = [pltpu.make_async_copy(wq_ref, wcat.at[:, 0:head], w_sem),
                pltpu.make_async_copy(wkv_ref, wcat.at[:, head:2 * head], w_sem)]
    for copy in w_copies:
        copy.start()

    def block(d):
        return pl.ds(pl.multiple_of(xor(tp, d) * rows, rows), rows)

    cw = width // AG_CHUNKS

    def cols(c, w=cw):
        return slice(c * w, (c + 1) * w)

    for copy in loads[:2]:
        copy.wait()
    square = jnp.zeros((rows, 1), jnp.float32)
    for c in range(AG_CHUNKS):
        v = x_ref[:, cols(c)].astype(jnp.float32)
        square = square + jnp.sum(v * v, axis=1, keepdims=True)
    inv = 1.0 / jnp.sqrt(square * (1.0 / width) + EPS)
    inv_ref[...] = jnp.broadcast_to(inv, inv_ref.shape)

    half = width // 2
    held = AG_CHUNKS // 2

    def turn(c):
        at = lax.rem(c + held * (1 - x), AG_CHUNKS) * cw
        return pl.ds(pl.multiple_of(at, cw), cw)

    def nx(c, d):
        if d & 1:
            part = normed_x.at[block(d ^ 1), cols(c)]
            return remote(part, part, nx_s.at[1], nx_r.at[held], "tp", 1)
        return remote(normed.at[block(d), turn(c)], normed_x.at[block(d), cols(c)],
                      nx_s.at[0], nx_r.at[c], "dp", 1)

    def nx_all(i, k, at):
        part = normed_x.at[0:length // 2, at]
        return remote(part, part, nx_s.at[i], nx_r.at[k], "tp", 1)

    def ag(c, d):
        b = low_bit(d)
        part = normed.at[block(d ^ b), turn(c)]
        return remote(part, part, ag_s.at[d], ag_r.at[c, d // 2 if b > 1 else 0], "tp", b)

    order = sorted(range(1, ntp), key=lambda d: -low_bit(d))
    for c in range(AG_CHUNKS):
        unit = x_ref[:, turn(c)].astype(jnp.float32) * inv
        normed[block(0), turn(c)] = (unit * gain_ref[:, turn(c)]).astype(jnp.bfloat16)
        if c == 0:
            pl.semaphore_wait(barrier, len(tp_bits) + len(dp_bits) + 2)
        for b in reversed(tp_bits):
            ag(c, b).start()
        if c < held:
            nx(c, 0).start()
    for copy in loads[2:]:
        copy.wait()
    pltpu.make_async_copy(wcat, wcat, w_sem).wait()
    proj = jnp.zeros((length, 2 * head), jnp.float32)

    def forward(c):
        for d in order:
            if low_bit(d) > 1:
                ag(c, d).wait_recv()
                for b in reversed(tp_bits):
                    if b < low_bit(d):
                        ag(c, d | b).start()
                if c < held:
                    nx(c, d).start()

    def arrive(c, proj):
        part = normed.at[0:length // 2, turn(c)]
        remote(part, part, ag_s.at[1], ag_r.at[c, 0], "tp", 1).wait_recv()
        return proj + dot(normed[:, turn(c)], wcat[turn(c), :], 1, 0)

    def share(i):
        nx_all(0, i, cols(i)).wait_recv()
        for d in range(0, ntp, 2):
            nx(i, d | 1).start()

    forward(0)
    for c in range(AG_CHUNKS):
        if c + 1 < AG_CHUNKS:
            forward(c + 1)
        if c == AG_CHUNKS - 1:
            for i in range(held - 1):
                share(i)
        proj = arrive(c, proj)

    odd = lax.rem(tp, 2) == 1
    cosine, sine = rope_ref[0], rope_ref[1]

    def rope(u):
        return u * cosine + pltpu.roll(u, head // 2, 1) * sine

    def rope_t(u):
        return u * cosine - pltpu.roll(u, head // 2, 1) * sine

    raw = proj[:, head:]
    own = jnp.where(odd, raw, rope(raw))
    kv_out[0] = own.astype(jnp.bfloat16)
    swap = remote(kv_out.at[0], kv_in.at[0], kv_s.at[0], kv_r.at[0], "tp", 1)
    swap.start()
    share(held - 1)
    query = rope(proj[:, :head]).astype(jnp.bfloat16)
    seg_s = jnp.broadcast_to(seg_ref[...].astype(jnp.float32), (length, length))
    seg_t = seg_s.T
    t_at = lax.broadcasted_iota(jnp.int32, (length, length), 0)
    s_at = lax.broadcasted_iota(jnp.int32, (length, length), 1)
    allowed = (t_at >= s_at) & (seg_s == seg_t)
    scale = head ** (-0.5)
    swap.wait_recv()
    mine, other = kv_out[0].astype(jnp.float32), kv_in[0].astype(jnp.float32)
    keys = jnp.where(odd, other, mine).astype(jnp.bfloat16)
    values = jnp.where(odd, mine, other).astype(jnp.bfloat16)
    cot = cot_ref[...]
    scores = jnp.where(allowed, dot(query, keys, 1, 1) * scale, jnp.float32(-1e30))
    top = jnp.max(scores, axis=1, keepdims=True)
    e = jnp.exp(scores - top)
    probs = e / jnp.sum(e, axis=1, keepdims=True)
    prob_grad = dot(cot, values, 1, 1)
    delta = jnp.sum(probs * prob_grad, axis=1, keepdims=True)
    score_grad = (probs * (prob_grad - delta) * scale).astype(jnp.bfloat16)
    grads[:, :head] = rope_t(dot(score_grad, keys, 1, 0)).astype(jnp.bfloat16)

    def gx(p):
        at = slice(p * head, (p + 1) * head)
        return remote(grads.at[:, at], grads_x.at[:, at], gx_s.at[p], gx_r.at[p], "dp", 1)

    gx(0).start()
    key_part = rope_t(dot(score_grad, query, 0, 0))
    value_part = dot(probs.astype(jnp.bfloat16), cot, 0, 0)
    kv_out[1] = jnp.where(odd, key_part, value_part).astype(jnp.bfloat16)
    swap = remote(kv_out.at[1], kv_in.at[1], kv_s.at[1], kv_r.at[1], "tp", 1)
    swap.start()
    own_grad = jnp.where(odd, value_part, key_part).astype(jnp.bfloat16).astype(jnp.float32)
    swap.wait_recv()
    grads[:, head:] = (own_grad + kv_in[1].astype(jnp.float32)).astype(jnp.bfloat16)
    gx(1).start()

    blocks = half // BLOCK
    chunks = 2 * blocks
    whole = (qg_ref, kvg_ref)

    def local_rows(q):
        at = (q % blocks) * BLOCK
        return slice(at, at + BLOCK)

    def mine_rows(q):
        return pl.ds(pl.multiple_of(x * half + (q % blocks) * BLOCK, BLOCK), BLOCK)

    def mine(q):
        return term.at[q // blocks, local_rows(q), :]

    def kind(q):
        return q // blocks

    def inward(q):
        if q == chunks:
            return to(gsum, gchain.at[is_middle], in_s.at[kind(q)], chain_r.at[is_middle, q], "dp", inner_dp)
        return to(mine(q), chain.at[q, is_middle], in_s.at[kind(q)], chain_r.at[is_middle, q], "dp", inner_dp)

    def arrived(q, slot):
        if q == chunks:
            return to(gsum, gchain.at[slot], in_s.at[kind(q)], chain_r.at[slot, q], "dp", inner_dp)
        return to(mine(q), chain.at[q, slot], in_s.at[kind(q)], chain_r.at[slot, q], "dp", inner_dp)

    half_at = pl.ds(pl.multiple_of(x * half, half), half)

    def result_part(q):
        if q == chunks:
            return gg_ref.at[:, half_at]
        return whole[q // blocks].at[mine_rows(q), :]

    def outward(q):
        part = result_part(q)
        return to(part, part, down_s.at[kind(q)], chain_r.at[1, q], "dp", outer_dp)

    def final(q):
        part = result_part(q)
        return remote(part, part, last_s.at[kind(q)], last_r.at[kind(q)], "dp", 1)

    def form(q):
        at = slice(q // blocks * head, (q // blocks + 1) * head)
        value = dot(normed[:, mine_rows(q)], grads[:, at], 0, 0)
        value = value + dot(normed_x[:, local_rows(q)], grads_x[:, at], 0, 0)
        term[q // blocks, local_rows(q), :] = value.astype(jnp.bfloat16)

        @pl.when(depth == 0)
        def _():
            inward(q).start()

        value = value * wcat[mine_rows(q), at].astype(jnp.float32)
        if q < blocks:
            weigh[local_rows(q), :] = value
        else:
            value = value + weigh[local_rows(q), :]
            gs[0, :, local_rows(q)] = jnp.sum(value.T, axis=0, keepdims=True)

    def plus(q, slot):
        value = term[q // blocks, local_rows(q), :].astype(jnp.float32)
        return (value + chain[q, slot].astype(jnp.float32)).astype(jnp.bfloat16)

    def gather(q):
        @pl.when(depth > 0)
        def _():
            arrived(q, 0).wait_recv()
            if q == chunks:
                gsum[...] = gsum[...] + gchain[0]
            else:
                term[q // blocks, local_rows(q), :] = plus(q, 0)
            inward(q).start()

    def turn_back(q):
        @pl.when(depth == middle)
        def _():
            arrived(q, 1).wait_recv()
            if q == chunks:
                gg_ref[:, half_at] = (gsum[...] + gchain[1]) / gain_ref[:, half_at]
            else:
                whole[q // blocks][mine_rows(q), :] = plus(q, 1)
            outward(q).start()
            final(q).start()

    def pass_on(q):
        @pl.when(depth < middle)
        def _():
            outward(q).wait_recv()

            @pl.when(depth > 0)
            def _():
                outward(q).start()

            final(q).start()

    rw = width // RS_CHUNKS
    rs_order = sorted(range(1, ntp), key=low_bit)

    def rs(c, d):
        return remote(rs_out.at[d, :, cols(c, rw)], rs_in.at[d, :, cols(c, rw)],
                      rs_s.at[tp_bits.index(low_bit(d))], rs_r.at[c, tp_bits.index(low_bit(d))],
                      "tp", low_bit(d))

    def rs_all(c, at, b):
        n = ntp // (2 * b)
        i = tp_bits.index(b)
        return remote(rs_out.at[0:n, :, at], rs_in.at[0:n, :, at], rs_s.at[i], rs_r.at[c, i], "tp", b)

    def partial(c, d):
        value = tot[block(d), cols(c, rw)]
        for b in tp_bits:
            if d == 0 or b < low_bit(d):
                value = value + rs_in[d | b, :, cols(c, rw)].astype(jnp.float32)
        return value

    def rs_send(c, b):
        for d in rs_order:
            if low_bit(d) == b:
                rs_out[d, :, cols(c, rw)] = partial(c, d).astype(jnp.bfloat16)
                rs(c, d).start()

    def rs_wait(c, b):
        rs_all(c, cols(c, rw), b).wait_recv()

    def back(c):
        tot[:, cols(c, rw)] = dot(grads[...], wcat[cols(c, rw), :], 1, 1)
        rs_send(c, 1)

    def rest(c, b):
        rs_wait(c, b // 2)
        rs_send(c, b)

    scale_back = inv_ref[:, 0:1]

    def exchange(k):
        return remote(gs.at[k], gr.at[k], g_s.at[k], g_r.at[k], "tp", tp_bits[k])

    def add_up(k):
        exchange(k).wait_recv()
        if k + 1 < len(tp_bits):
            gs[k + 1] = gs[k] + gr[k]
            exchange(k + 1).start()
        else:
            gsum[...] = gs[k] + gr[k]

            @pl.when(depth == 0)
            def _():
                inward(chunks).start()

    inner = [jnp.zeros((rows, 1), jnp.float32)]

    def unit(c):
        return x_ref[:, cols(c, rw)].astype(jnp.float32) * scale_back

    def project(c):
        rs_wait(c, tp_bits[-1])
        scaled = partial(c, 0) * gain_ref[:, cols(c, rw)]
        tot[block(0), cols(c, rw)] = scaled
        inner[0] = inner[0] + jnp.sum(scaled * unit(c), axis=1, keepdims=True)

    def result(c):
        scaled = tot[block(0), cols(c, rw)]
        ig_ref[:, cols(c, rw)] = ((scaled - unit(c) * (inner[0] * (1.0 / width))) * scale_back).astype(jnp.bfloat16)

    work = []

    def later(step, f, *args):
        work.append((step, len(work), functools.partial(f, *args)))

    for c in range(FIRST_BACK):
        back(c)
    nx_all(1, held, slice(0, half)).wait_recv()
    gx(0).wait_recv()
    for q in range(blocks):
        form(q)
    for c in range(FIRST_BACK, RS_CHUNKS):
        later(c - FIRST_BACK, back, c)
    later(FORM_AT, lambda: gx(1).wait_recv())
    for q in range(blocks, chunks):
        at = FORM_AT + (q - blocks) // FORMS
        later(at, form, q)
    later(at, lambda: exchange(0).start())
    for k in range(len(tp_bits)):
        later(at + GAIN_EVERY * (k + 1), add_up, k)
    at = max(GAIN_AT, at + GAIN_EVERY * len(tp_bits) + 1)
    later(at, gather, chunks)
    later(at + MIDDLE_LAG, turn_back, chunks)
    later(at + OUTER_LAG, pass_on, chunks)
    for i, b in enumerate(tp_bits[1:]):
        for c in range(RS_CHUNKS):
            later(REST_AT + i * RS_CHUNKS + c, rest, c, b)
    at = LAST_AT + (len(tp_bits) - 2) * RS_CHUNKS
    for c in range(RS_CHUNKS):
        later(at + 2 * c, project, c)
    for c in range(RS_CHUNKS):
        later(at + 2 * RS_CHUNKS + c, result, c)
    work.sort(key=lambda w: w[:2])
    for step in range(chunks + max(OUTER_LAG, MIDDLE_LAG)):
        if step < chunks:
            gather(step)
        if 0 <= step - MIDDLE_LAG < chunks:
            turn_back(step - MIDDLE_LAG)
        if 0 <= step - OUTER_LAG < chunks:
            pass_on(step - OUTER_LAG)
        while work and work[0][0] <= step:
            work.pop(0)[2]()
    for _, _, f in work:
        f()

    def whole_kind(i, copy):
        if i == 2:
            return copy(gsum, gg_ref.at[:, half_at])
        return copy(term.at[i], whole[i].at[half_at, :])

    for i in range(3):
        whole_kind(i, lambda a, b: remote(b, b, last_s.at[i], last_r.at[i], "dp", 1)).wait()
        whole_kind(i, lambda a, b: to(a, a, in_s.at[i], chain_r.at[0, 0], "dp", inner_dp)).wait_send()

    @pl.when(depth > 0)
    def _():
        for i in range(3):
            whole_kind(i, lambda a, b: to(b, b, down_s.at[i], chain_r.at[1, 0], "dp", outer_dp)).wait_send()

    for d in range(1, ntp):
        part = normed.at[block(0), :]
        remote(part, part, ag_s.at[d], ag_r.at[0, 0], "tp", 1).wait_send()
    for i in range(2):
        nx_all(i, held, slice(0, half)).wait_send()
        gx(i).wait_send()
        remote(kv_out.at[i], kv_in.at[i], kv_s.at[i], kv_r.at[i], "tp", 1).wait_send()
    for b in tp_bits:
        rs_all(0, slice(0, width), b).wait_send()
        exchange(tp_bits.index(b)).wait_send()


def store(*refs):
    copies = [pltpu.make_async_copy(refs[i], refs[4 + i], refs[8].at[i]) for i in range(4)]
    for copy in copies:
        copy.start()
    for copy in copies:
        copy.wait()


def on_device(ntp, ndp, activations, cotangent, segment_ids, norm_gain, query_weight, key_value_weight):
    rows, width = activations.shape
    length, head = cotangent.shape
    angle = np.arange(length)[:, None] * 500000.0 ** (-np.arange(0, head, 2) / head)[None, :]
    cosine = np.concatenate([np.cos(angle), np.cos(angle)], axis=1).astype(np.float32)
    sine = np.concatenate([-np.sin(angle), np.sin(angle)], axis=1).astype(np.float32)
    chunks = width // BLOCK
    nb = len(bits_of(ntp))
    bf, f32 = jnp.bfloat16, jnp.float32
    vmem = pl.BlockSpec(memory_space=pltpu.VMEM)
    anywhere = pl.BlockSpec(memory_space=pl.ANY)
    hbm = pl.BlockSpec(memory_space=pltpu.HBM)
    dma = pltpu.SemaphoreType.DMA
    outs = pl.pallas_call(
        functools.partial(kernel, ntp, ndp),
        out_shape=[
            pltpu.VMEM((rows, width), bf),
            pltpu.VMEM((width, head), bf),
            pltpu.VMEM((width, head), bf),
            pltpu.VMEM((1, width), f32),
        ],
        in_specs=[hbm] * 7,
        out_specs=[vmem, vmem, vmem, vmem],
        scratch_shapes=[
            pltpu.VMEM((width, 2 * head), bf),
            pltpu.VMEM((length, width), bf),
            pltpu.VMEM((length, width // 2), bf),
            pltpu.VMEM((length, 2 * head), bf),
            pltpu.VMEM((length, 2 * head), bf),
            pltpu.VMEM((length, width), f32),
            pltpu.VMEM((ntp, rows, width), bf),
            pltpu.VMEM((ntp, rows, width), bf),
            pltpu.VMEM((2, width // 2, head), bf),
            pltpu.VMEM((chunks, 2, BLOCK, head), bf),
            pltpu.VMEM((width // 2, head), f32),
            pltpu.VMEM((nb, 1, width // 2), f32),
            pltpu.VMEM((nb, 1, width // 2), f32),
            pltpu.VMEM((1, width // 2), f32),
            pltpu.VMEM((2, 1, width // 2), f32),
            pltpu.VMEM((2, length, head), bf),
            pltpu.VMEM((2, length, head), bf),
            pltpu.VMEM((rows, 128), f32),
            dma,
            dma((ntp,)),
            dma((AG_CHUNKS, ntp // 2)),
            dma((2,)),
            dma((AG_CHUNKS // 2 + 1,)),
            dma((2,)),
            dma((2,)),
            dma((nb,)),
            dma((RS_CHUNKS, nb)),
            dma((3,)),
            dma((2, chunks + 1)),
            dma((3,)),
            dma((3,)),
            dma((3,)),
            dma((nb,)),
            dma((nb,)),
            dma((2,)),
            dma((2,)),
            pltpu.VMEM((rows, width), bf),
            pltpu.VMEM((length, head), bf),
            pltpu.VMEM((1, length), jnp.int32),
            pltpu.VMEM((1, width), f32),
            pltpu.VMEM((2, length, head), f32),
            dma((5,)),
        ],
        compiler_params=pltpu.CompilerParams(
            collective_id=0, has_side_effects=True, vmem_limit_bytes=40 * 1024 * 1024),
    )(*[pltpu.with_memory_space_constraint(v, pltpu.HBM) for v in (
        activations, cotangent, segment_ids.reshape(1, length), norm_gain.reshape(1, width),
        jnp.asarray(np.stack([cosine, sine])), query_weight, key_value_weight)])
    outs = pl.pallas_call(
        store,
        out_shape=[
            jax.ShapeDtypeStruct((rows, width), bf),
            jax.ShapeDtypeStruct((width, head), bf),
            jax.ShapeDtypeStruct((width, head), bf),
            jax.ShapeDtypeStruct((1, width), f32),
        ],
        in_specs=[vmem] * 4,
        out_specs=[hbm] * 4,
        scratch_shapes=[dma((4,))],
    )(*[pltpu.with_memory_space_constraint(v, pltpu.VMEM) for v in outs])
    return (outs[0], outs[1], outs[2], outs[3].reshape(width))


def solution(mesh):
    return jax.shard_map(
        functools.partial(on_device, mesh.shape["tp"], mesh.shape["dp"]),
        mesh=mesh,
        in_specs=(P(("dp", "tp"), None), P("dp", "tp"), P("dp"), P(), P(None, "tp"), P(None, "tp")),
        out_specs=(P(("dp", "tp"), None), P(None, "tp"), P(None, "tp"), P()),
        check_vma=False,
    )
```

```python
import functools

import jax
import jax.numpy as jnp
import numpy as np
from jax import lax
from jax.experimental import pallas as pl
from jax.experimental.pallas import tpu as pltpu
from jax.sharding import PartitionSpec as P

EPS = 1e-05
AG_CHUNKS = 4
BLOCK = 128
OUTER_LAG, MIDDLE_LAG = 10, 4
RS_CHUNKS = 8
QUERY_FORMS = (1, 3, 4, 8)
FIRST_BACK, FORM_AT, FORM_EVERY, FORMS, REST_AT, LAST_AT, GAIN_EVERY, GAIN_AT = 2, 2, 2, 2, 10, 18, 5, 30


def low_bit(d):
    return d & -d


def bits_of(n):
    return [1 << k for k in range(n.bit_length() - 1)]


def bit_at(v, b):
    return lax.rem(lax.div(v, b), 2)


def xor(v, mask):
    out = v
    for b in bits_of(1 << mask.bit_length()):
        if mask & b:
            out = out + b - 2 * b * bit_at(v, b)
    return out


def dot(a, b, ca, cb):
    return lax.dot_general(a, b, (((ca,), (cb,)), ((), ())), preferred_element_type=jnp.float32)


def kernel(ntp, ndp, x_hbm, cot_hbm, seg_hbm, gain_hbm, rope_hbm, wq_ref, wkv_ref,
           ig_ref, qg_ref, kvg_ref, gg_ref,
           wcat, normed, normed_x, normed_t, both, tot, rs_out, rs_in, term, chain, weigh, gs, gr, gsum, gchain,
           kv_out, kv_in, inv_ref,
           w_sem, ag_s, ag_r, nx_s, nx_r, gx_s, gx_r, rs_s, rs_r, in_s, chain_r, down_s,
           last_s, last_r, g_s, g_r, kv_s, kv_r,
           x_ref, cot_ref, seg_ref, gain_ref, rope_ref, load_sem):
    tp, dp = lax.axis_index("tp"), lax.axis_index("dp")
    tp_bits, dp_bits = bits_of(ntp), bits_of(ndp)
    rows, width = x_ref.shape
    length = cot_ref.shape[0]
    grads, grads_x = both.at[0:length, :], both.at[length:2 * length, :]
    head = cot_ref.shape[1]
    x, z, deep = lax.rem(dp, 2), lax.div(dp, 2), ndp // 2
    middle = deep // 2 - 1
    side = lax.div(z, deep // 2)
    depth = z + side * (deep - 1 - 2 * z)
    inner_dp = dp + 2 * (1 - 2 * side)
    outer_dp = dp - 2 * (1 - 2 * side)
    is_middle = lax.div(depth, middle) if middle else 1

    def to(src, dst, s, r, axis, device):
        return pltpu.make_async_remote_copy(
            src_ref=src, dst_ref=dst, send_sem=s, recv_sem=r,
            device_id={axis: device}, device_id_type=pl.DeviceIdType.MESH)

    def remote(src, dst, s, r, axis, b):
        return to(src, dst, s, r, axis, xor(tp if axis == "tp" else dp, b))

    loads = [pltpu.make_async_copy(src, dst, load_sem.at[i]) for i, (src, dst) in enumerate((
        (x_hbm, x_ref), (gain_hbm, gain_ref), (cot_hbm, cot_ref), (seg_hbm, seg_ref),
        (rope_hbm, rope_ref)))]
    for copy in loads:
        copy.start()
    barrier = pltpu.get_barrier_semaphore()
    for b in tp_bits:
        pl.semaphore_signal(barrier, inc=1, device_id={"tp": xor(tp, b)},
                            device_id_type=pl.DeviceIdType.MESH)
    for b in dp_bits:
        pl.semaphore_signal(barrier, inc=1, device_id={"dp": xor(dp, b)},
                            device_id_type=pl.DeviceIdType.MESH)

    for step in (2, ndp - 2):
        pl.semaphore_signal(barrier, inc=1, device_id={"dp": lax.rem(dp + step, ndp)},
                            device_id_type=pl.DeviceIdType.MESH)

    w_copies = [pltpu.make_async_copy(wq_ref, wcat.at[:, 0:head], w_sem),
                pltpu.make_async_copy(wkv_ref, wcat.at[:, head:2 * head], w_sem)]
    for copy in w_copies:
        copy.start()

    def block(d):
        return pl.ds(pl.multiple_of(xor(tp, d) * rows, rows), rows)

    cw = width // AG_CHUNKS

    def cols(c, w=cw):
        return slice(c * w, (c + 1) * w)

    for copy in loads[:2]:
        copy.wait()
    square = jnp.zeros((rows, 1), jnp.float32)
    for c in range(AG_CHUNKS):
        v = x_ref[:, cols(c)].astype(jnp.float32)
        square = square + jnp.sum(v * v, axis=1, keepdims=True)
    inv = 1.0 / jnp.sqrt(square * (1.0 / width) + EPS)
    inv_ref[...] = jnp.broadcast_to(inv, inv_ref.shape)

    half = width // 2
    held = AG_CHUNKS // 2

    def turn(c):
        at = lax.rem(c + held * (1 - x), AG_CHUNKS) * cw
        return pl.ds(pl.multiple_of(at, cw), cw)

    def nx(c, d):
        if d & 1:
            part = normed_x.at[block(d ^ 1), cols(c)]
            return remote(part, part, nx_s.at[1], nx_r.at[held], "tp", 1)
        return remote(normed.at[block(d), turn(c)], normed_x.at[block(d), cols(c)],
                      nx_s.at[0], nx_r.at[c], "dp", 1)

    def nx_all(i, k, at):
        part = normed_x.at[0:length // 2, at]
        return remote(part, part, nx_s.at[i], nx_r.at[k], "tp", 1)

    def ag(c, d):
        b = low_bit(d)
        part = normed.at[block(d ^ b), turn(c)]
        return remote(part, part, ag_s.at[d], ag_r.at[c, d // 2 if b > 1 else 0], "tp", b)

    order = sorted(range(1, ntp), key=lambda d: -low_bit(d))
    for c in range(AG_CHUNKS):
        unit = x_ref[:, turn(c)].astype(jnp.float32) * inv
        normed[block(0), turn(c)] = (unit * gain_ref[:, turn(c)]).astype(jnp.bfloat16)
        if c == 0:
            pl.semaphore_wait(barrier, len(tp_bits) + len(dp_bits) + 2)
        for b in reversed(tp_bits):
            ag(c, b).start()
        if c < held:
            nx(c, 0).start()
    for copy in loads[2:]:
        copy.wait()
    pltpu.make_async_copy(wcat, wcat, w_sem).wait()
    proj = jnp.zeros((length, 2 * head), jnp.float32)

    def forward(c):
        for d in order:
            if low_bit(d) > 1:
                ag(c, d).wait_recv()
                for b in reversed(tp_bits):
                    if b < low_bit(d):
                        ag(c, d | b).start()
                if c < held:
                    nx(c, d).start()

    def arrive(c, proj):
        part = normed.at[0:length // 2, turn(c)]
        remote(part, part, ag_s.at[1], ag_r.at[c, 0], "tp", 1).wait_recv()
        value = normed[:, turn(c)]
        if c >= held:
            normed_t[cols(c - held), 0:length] = value.T
        return proj + dot(value, wcat[turn(c), :], 1, 0)

    def share(i):
        nx_all(0, i, cols(i)).wait_recv()
        for d in range(0, ntp, 2):
            nx(i, d | 1).start()

    forward(0)
    for c in range(AG_CHUNKS):
        if c + 1 < AG_CHUNKS:
            forward(c + 1)
        if c == AG_CHUNKS - 1:
            for i in range(held - 1):
                share(i)
        proj = arrive(c, proj)

    odd = lax.rem(tp, 2) == 1
    cosine, sine = rope_ref[0], rope_ref[1]

    def rope(u):
        return u * cosine + pltpu.roll(u, head // 2, 1) * sine

    def rope_t(u):
        return u * cosine - pltpu.roll(u, head // 2, 1) * sine

    raw = proj[:, head:]
    own = jnp.where(odd, raw, rope(raw))
    kv_out[0] = own.astype(jnp.bfloat16)
    swap = remote(kv_out.at[0], kv_in.at[0], kv_s.at[0], kv_r.at[0], "tp", 1)
    swap.start()
    share(held - 1)
    query = rope(proj[:, :head]).astype(jnp.bfloat16)
    seg_s = jnp.broadcast_to(seg_ref[...].astype(jnp.float32), (length, length))
    seg_t = seg_s.T
    t_at = lax.broadcasted_iota(jnp.int32, (length, length), 0)
    s_at = lax.broadcasted_iota(jnp.int32, (length, length), 1)
    allowed = (t_at >= s_at) & (seg_s == seg_t)
    scale = head ** (-0.5)
    swap.wait_recv()
    mine, other = kv_out[0].astype(jnp.float32), kv_in[0].astype(jnp.float32)
    keys = jnp.where(odd, other, mine).astype(jnp.bfloat16)
    values = jnp.where(odd, mine, other).astype(jnp.bfloat16)
    cot = cot_ref[...]
    scores = jnp.where(allowed, dot(query, keys, 1, 1) * scale, jnp.float32(-1e30))
    top = jnp.max(scores, axis=1, keepdims=True)
    e = jnp.exp(scores - top)
    probs = e / jnp.sum(e, axis=1, keepdims=True)
    prob_grad = dot(cot, values, 1, 1)
    delta = jnp.sum(probs * prob_grad, axis=1, keepdims=True)
    score_grad = (probs * (prob_grad - delta) * scale).astype(jnp.bfloat16)
    grads[:, :head] = rope_t(dot(score_grad, keys, 1, 0)).astype(jnp.bfloat16)

    def gx(p):
        at = slice(p * head, (p + 1) * head)
        return remote(grads.at[:, at], grads_x.at[:, at], gx_s.at[p], gx_r.at[p], "dp", 1)

    gx(0).start()
    key_part = rope_t(dot(score_grad, query, 0, 0))
    value_part = dot(probs.astype(jnp.bfloat16), cot, 0, 0)
    kv_out[1] = jnp.where(odd, key_part, value_part).astype(jnp.bfloat16)
    swap = remote(kv_out.at[1], kv_in.at[1], kv_s.at[1], kv_r.at[1], "tp", 1)
    swap.start()
    own_grad = jnp.where(odd, value_part, key_part).astype(jnp.bfloat16).astype(jnp.float32)
    swap.wait_recv()
    grads[:, head:] = (own_grad + kv_in[1].astype(jnp.float32)).astype(jnp.bfloat16)
    gx(1).start()

    blocks = half // BLOCK
    chunks = 2 * blocks
    whole = (qg_ref, kvg_ref)

    def local_rows(q):
        at = (q % blocks) * BLOCK
        return slice(at, at + BLOCK)

    def mine_rows(q):
        return pl.ds(pl.multiple_of(x * half + (q % blocks) * BLOCK, BLOCK), BLOCK)

    def mine(q):
        return term.at[q // blocks, local_rows(q), :]

    def kind(q):
        return q // blocks

    def inward(q):
        if q == chunks:
            return to(gsum, gchain.at[is_middle], in_s.at[kind(q)], chain_r.at[is_middle, q], "dp", inner_dp)
        return to(mine(q), chain.at[q, is_middle], in_s.at[kind(q)], chain_r.at[is_middle, q], "dp", inner_dp)

    def arrived(q, slot):
        if q == chunks:
            return to(gsum, gchain.at[slot], in_s.at[kind(q)], chain_r.at[slot, q], "dp", inner_dp)
        return to(mine(q), chain.at[q, slot], in_s.at[kind(q)], chain_r.at[slot, q], "dp", inner_dp)

    half_at = pl.ds(pl.multiple_of(x * half, half), half)

    def result_part(q):
        if q == chunks:
            return gg_ref.at[:, half_at]
        return whole[q // blocks].at[mine_rows(q), :]

    def outward(q):
        part = result_part(q)
        return to(part, part, down_s.at[kind(q)], chain_r.at[1, q], "dp", outer_dp)

    def final(q):
        part = result_part(q)
        return remote(part, part, last_s.at[kind(q)], last_r.at[kind(q)], "dp", 1)

    def form(q, n):
        p = q // blocks
        at = slice(p * head, (p + 1) * head)
        local = slice(q % blocks * BLOCK, (q % blocks + n) * BLOCK)
        value = dot(normed_t[local, :], both[:, at], 1, 0)
        term[p, local, :] = value.astype(jnp.bfloat16)

        @pl.when(depth == 0)
        def _():
            for i in range(n):
                inward(q + i).start()

        rows_here = pl.ds(pl.multiple_of(x * half + q % blocks * BLOCK, BLOCK), n * BLOCK)
        value = value * wcat[rows_here, at].astype(jnp.float32)
        if p == 0:
            weigh[local, :] = value
        else:
            value = value + weigh[local, :]
            gs[0, :, local] = jnp.sum(value.T, axis=0, keepdims=True)

    def plus(q, slot):
        value = term[q // blocks, local_rows(q), :].astype(jnp.float32)
        return (value + chain[q, slot].astype(jnp.float32)).astype(jnp.bfloat16)

    def gather(q):
        @pl.when(depth > 0)
        def _():
            arrived(q, 0).wait_recv()
            if q == chunks:
                gsum[...] = gsum[...] + gchain[0]
            else:
                term[q // blocks, local_rows(q), :] = plus(q, 0)
            inward(q).start()

    def turn_back(q):
        @pl.when(depth == middle)
        def _():
            arrived(q, 1).wait_recv()
            if q == chunks:
                gg_ref[:, half_at] = (gsum[...] + gchain[1]) / gain_ref[:, half_at]
            else:
                whole[q // blocks][mine_rows(q), :] = plus(q, 1)
            outward(q).start()
            final(q).start()

    def pass_on(q):
        @pl.when(depth < middle)
        def _():
            outward(q).wait_recv()

            @pl.when(depth > 0)
            def _():
                outward(q).start()

            final(q).start()

    rw = width // RS_CHUNKS
    rs_order = sorted(range(1, ntp), key=low_bit)

    def rs(c, d):
        return remote(rs_out.at[d, :, cols(c, rw)], rs_in.at[d, :, cols(c, rw)],
                      rs_s.at[tp_bits.index(low_bit(d))], rs_r.at[c, tp_bits.index(low_bit(d))],
                      "tp", low_bit(d))

    def rs_all(c, at, b):
        n = ntp // (2 * b)
        i = tp_bits.index(b)
        return remote(rs_out.at[0:n, :, at], rs_in.at[0:n, :, at], rs_s.at[i], rs_r.at[c, i], "tp", b)

    def partial(c, d):
        value = tot[block(d), cols(c, rw)]
        for b in tp_bits:
            if d == 0 or b < low_bit(d):
                value = value + rs_in[d | b, :, cols(c, rw)].astype(jnp.float32)
        return value

    def rs_send(c, b):
        for d in rs_order:
            if low_bit(d) == b:
                rs_out[d, :, cols(c, rw)] = partial(c, d).astype(jnp.bfloat16)
                rs(c, d).start()

    def rs_wait(c, b):
        rs_all(c, cols(c, rw), b).wait_recv()

    def back(c):
        tot[:, cols(c, rw)] = dot(grads[...], wcat[cols(c, rw), :], 1, 1)
        rs_send(c, 1)

    def rest(c, b):
        rs_wait(c, b // 2)
        rs_send(c, b)

    scale_back = inv_ref[:, 0:1]

    def exchange(k):
        return remote(gs.at[k], gr.at[k], g_s.at[k], g_r.at[k], "tp", tp_bits[k])

    def add_up(k):
        exchange(k).wait_recv()
        if k + 1 < len(tp_bits):
            gs[k + 1] = gs[k] + gr[k]
            exchange(k + 1).start()
        else:
            gsum[...] = gs[k] + gr[k]

            @pl.when(depth == 0)
            def _():
                inward(chunks).start()

    inner = [jnp.zeros((rows, 1), jnp.float32)]

    def unit(c):
        return x_ref[:, cols(c, rw)].astype(jnp.float32) * scale_back

    def project(c):
        rs_wait(c, tp_bits[-1])
        scaled = partial(c, 0) * gain_ref[:, cols(c, rw)]
        tot[block(0), cols(c, rw)] = scaled
        inner[0] = inner[0] + jnp.sum(scaled * unit(c), axis=1, keepdims=True)

    def result(c):
        scaled = tot[block(0), cols(c, rw)]
        ig_ref[:, cols(c, rw)] = ((scaled - unit(c) * (inner[0] * (1.0 / width))) * scale_back).astype(jnp.bfloat16)

    work = []

    def later(step, f, *args):
        work.append((step, len(work), functools.partial(f, *args)))

    for c in range(FIRST_BACK):
        back(c)
    nx_all(1, held, slice(0, half)).wait_recv()
    for i in range(held):
        normed_t[cols(i), length:2 * length] = normed_x[:, cols(i)].T
    gx(0).wait_recv()
    q = 0
    for n in QUERY_FORMS:
        form(q, n)
        q = q + n
    for c in range(FIRST_BACK, RS_CHUNKS):
        later(c - FIRST_BACK, back, c)
    later(FORM_AT, lambda: gx(1).wait_recv())
    for i in range(blocks // FORMS):
        at = FORM_AT + FORM_EVERY * i
        later(at, form, blocks + FORMS * i, FORMS)
    later(at, lambda: exchange(0).start())
    for k in range(len(tp_bits)):
        later(at + GAIN_EVERY * (k + 1), add_up, k)
    at = max(GAIN_AT, at + GAIN_EVERY * len(tp_bits) + 1)
    later(at, gather, chunks)
    later(at + MIDDLE_LAG, turn_back, chunks)
    later(at + OUTER_LAG, pass_on, chunks)
    for i, b in enumerate(tp_bits[1:]):
        for c in range(RS_CHUNKS):
            later(REST_AT + i * RS_CHUNKS + c, rest, c, b)
    at = LAST_AT + (len(tp_bits) - 2) * RS_CHUNKS
    for c in range(RS_CHUNKS):
        later(at + 2 * c, project, c)
    for c in range(RS_CHUNKS):
        later(at + 2 * RS_CHUNKS + c, result, c)
    work.sort(key=lambda w: w[:2])
    for step in range(chunks + max(OUTER_LAG, MIDDLE_LAG)):
        if step < chunks:
            gather(step)
        if 0 <= step - MIDDLE_LAG < chunks:
            turn_back(step - MIDDLE_LAG)
        if 0 <= step - OUTER_LAG < chunks:
            pass_on(step - OUTER_LAG)
        while work and work[0][0] <= step:
            work.pop(0)[2]()
    for _, _, f in work:
        f()

    def whole_kind(i, copy):
        if i == 2:
            return copy(gsum, gg_ref.at[:, half_at])
        return copy(term.at[i], whole[i].at[half_at, :])

    for i in range(3):
        whole_kind(i, lambda a, b: remote(b, b, last_s.at[i], last_r.at[i], "dp", 1)).wait()
        whole_kind(i, lambda a, b: to(a, a, in_s.at[i], chain_r.at[0, 0], "dp", inner_dp)).wait_send()

    @pl.when(depth > 0)
    def _():
        for i in range(3):
            whole_kind(i, lambda a, b: to(b, b, down_s.at[i], chain_r.at[1, 0], "dp", outer_dp)).wait_send()

    for d in range(1, ntp):
        part = normed.at[block(0), :]
        remote(part, part, ag_s.at[d], ag_r.at[0, 0], "tp", 1).wait_send()
    for i in range(2):
        nx_all(i, held, slice(0, half)).wait_send()
        gx(i).wait_send()
        remote(kv_out.at[i], kv_in.at[i], kv_s.at[i], kv_r.at[i], "tp", 1).wait_send()
    for b in tp_bits:
        rs_all(0, slice(0, width), b).wait_send()
        exchange(tp_bits.index(b)).wait_send()


def store(*refs):
    copies = [pltpu.make_async_copy(refs[i], refs[4 + i], refs[8].at[i]) for i in range(4)]
    for copy in copies:
        copy.start()
    for copy in copies:
        copy.wait()


def on_device(ntp, ndp, activations, cotangent, segment_ids, norm_gain, query_weight, key_value_weight):
    rows, width = activations.shape
    length, head = cotangent.shape
    angle = np.arange(length)[:, None] * 500000.0 ** (-np.arange(0, head, 2) / head)[None, :]
    cosine = np.concatenate([np.cos(angle), np.cos(angle)], axis=1).astype(np.float32)
    sine = np.concatenate([-np.sin(angle), np.sin(angle)], axis=1).astype(np.float32)
    chunks = width // BLOCK
    nb = len(bits_of(ntp))
    bf, f32 = jnp.bfloat16, jnp.float32
    vmem = pl.BlockSpec(memory_space=pltpu.VMEM)
    anywhere = pl.BlockSpec(memory_space=pl.ANY)
    hbm = pl.BlockSpec(memory_space=pltpu.HBM)
    dma = pltpu.SemaphoreType.DMA
    outs = pl.pallas_call(
        functools.partial(kernel, ntp, ndp),
        out_shape=[
            pltpu.VMEM((rows, width), bf),
            pltpu.VMEM((width, head), bf),
            pltpu.VMEM((width, head), bf),
            pltpu.VMEM((1, width), f32),
        ],
        in_specs=[hbm] * 7,
        out_specs=[vmem, vmem, vmem, vmem],
        scratch_shapes=[
            pltpu.VMEM((width, 2 * head), bf),
            pltpu.VMEM((length, width), bf),
            pltpu.VMEM((length, width // 2), bf),
            pltpu.VMEM((width // 2, 2 * length), bf),
            pltpu.VMEM((2 * length, 2 * head), bf),
            pltpu.VMEM((length, width), f32),
            pltpu.VMEM((ntp, rows, width), bf),
            pltpu.VMEM((ntp, rows, width), bf),
            pltpu.VMEM((2, width // 2, head), bf),
            pltpu.VMEM((chunks, 2, BLOCK, head), bf),
            pltpu.VMEM((width // 2, head), f32),
            pltpu.VMEM((nb, 1, width // 2), f32),
            pltpu.VMEM((nb, 1, width // 2), f32),
            pltpu.VMEM((1, width // 2), f32),
            pltpu.VMEM((2, 1, width // 2), f32),
            pltpu.VMEM((2, length, head), bf),
            pltpu.VMEM((2, length, head), bf),
            pltpu.VMEM((rows, 128), f32),
            dma,
            dma((ntp,)),
            dma((AG_CHUNKS, ntp // 2)),
            dma((2,)),
            dma((AG_CHUNKS // 2 + 1,)),
            dma((2,)),
            dma((2,)),
            dma((nb,)),
            dma((RS_CHUNKS, nb)),
            dma((3,)),
            dma((2, chunks + 1)),
            dma((3,)),
            dma((3,)),
            dma((3,)),
            dma((nb,)),
            dma((nb,)),
            dma((2,)),
            dma((2,)),
            pltpu.VMEM((rows, width), bf),
            pltpu.VMEM((length, head), bf),
            pltpu.VMEM((1, length), jnp.int32),
            pltpu.VMEM((1, width), f32),
            pltpu.VMEM((2, length, head), f32),
            dma((5,)),
        ],
        compiler_params=pltpu.CompilerParams(
            collective_id=0, has_side_effects=True, vmem_limit_bytes=40 * 1024 * 1024),
    )(*[pltpu.with_memory_space_constraint(v, pltpu.HBM) for v in (
        activations, cotangent, segment_ids.reshape(1, length), norm_gain.reshape(1, width),
        jnp.asarray(np.stack([cosine, sine])), query_weight, key_value_weight)])
    outs = pl.pallas_call(
        store,
        out_shape=[
            jax.ShapeDtypeStruct((rows, width), bf),
            jax.ShapeDtypeStruct((width, head), bf),
            jax.ShapeDtypeStruct((width, head), bf),
            jax.ShapeDtypeStruct((1, width), f32),
        ],
        in_specs=[vmem] * 4,
        out_specs=[hbm] * 4,
        scratch_shapes=[dma((4,))],
    )(*[pltpu.with_memory_space_constraint(v, pltpu.VMEM) for v in outs])
    return (outs[0], outs[1], outs[2], outs[3].reshape(width))


def solution(mesh):
    return jax.shard_map(
        functools.partial(on_device, mesh.shape["tp"], mesh.shape["dp"]),
        mesh=mesh,
        in_specs=(P(("dp", "tp"), None), P("dp", "tp"), P("dp"), P(), P(None, "tp"), P(None, "tp")),
        out_specs=(P(("dp", "tp"), None), P(None, "tp"), P(None, "tp"), P()),
        check_vma=False,
    )
```

```python
import functools

import jax
import jax.numpy as jnp
import numpy as np
from jax import lax
from jax.experimental import pallas as pl
from jax.experimental.pallas import tpu as pltpu
from jax.sharding import PartitionSpec as P

EPS = 1e-05
AG_CHUNKS = 4
BLOCK = 128
OUTER_LAG, MIDDLE_LAG = 10, 4
RS_CHUNKS = 8
EARLY = 2
QUERY_FORMS = (1, 3, 4, 6)
FIRST_BACK, FORM_AT, FORM_EVERY, FORMS, REST_AT, LAST_AT, GAIN_EVERY, GAIN_AT, EARLY_END = 1, 2, 2, 2, 10, 18, 5, 29, 26


def low_bit(d):
    return d & -d


def bits_of(n):
    return [1 << k for k in range(n.bit_length() - 1)]


def bit_at(v, b):
    return lax.rem(lax.div(v, b), 2)


def xor(v, mask):
    out = v
    for b in bits_of(1 << mask.bit_length()):
        if mask & b:
            out = out + b - 2 * b * bit_at(v, b)
    return out


def dot(a, b, ca, cb):
    return lax.dot_general(a, b, (((ca,), (cb,)), ((), ())), preferred_element_type=jnp.float32)


def kernel(ntp, ndp, x_hbm, cot_hbm, seg_hbm, gain_hbm, rope_hbm, wq_ref, wkv_ref,
           ig_ref, qg_ref, kvg_ref, gg_ref,
           wcat, normed, normed_x, normed_t, both, tot, rs_out, rs_in, term, chain, term_e, whole_e, seen_e, weigh, gs, gr, gsum, gchain,
           kv_out, kv_in, inv_ref,
           w_sem, ag_s, ag_r, nx_s, nx_r, gx_s, gx_r, rs_s, rs_r, in_s, chain_r, down_s,
           last_s, last_r, g_s, g_r, kv_s, kv_r, wx_s, wx_r,
           keep, x_ref, cot_ref, seg_ref, gain_ref, rope_ref, load_sem):
    tp, dp = lax.axis_index("tp"), lax.axis_index("dp")
    tp_bits, dp_bits = bits_of(ntp), bits_of(ndp)
    rows, width = x_ref.shape
    length = cot_ref.shape[0]
    grads, grads_x = both.at[0:length, :], both.at[length:2 * length, :]
    head = cot_ref.shape[1]
    x, z, deep = lax.rem(dp, 2), lax.div(dp, 2), ndp // 2
    middle = deep // 2 - 1
    side = lax.div(z, deep // 2)
    depth = z + side * (deep - 1 - 2 * z)
    inner_dp = dp + 2 * (1 - 2 * side)
    outer_dp = dp - 2 * (1 - 2 * side)
    is_middle = lax.div(depth, middle) if middle else 1

    def to(src, dst, s, r, axis, device):
        return pltpu.make_async_remote_copy(
            src_ref=src, dst_ref=dst, send_sem=s, recv_sem=r,
            device_id={axis: device}, device_id_type=pl.DeviceIdType.MESH)

    def remote(src, dst, s, r, axis, b):
        return to(src, dst, s, r, axis, xor(tp if axis == "tp" else dp, b))

    loads = [pltpu.make_async_copy(src, dst, load_sem.at[i]) for i, (src, dst) in enumerate((
        (x_hbm, x_ref), (gain_hbm, gain_ref), (cot_hbm, cot_ref), (seg_hbm, seg_ref),
        (rope_hbm, rope_ref)))]
    for copy in loads:
        copy.start()
    barrier = pltpu.get_barrier_semaphore()
    for b in tp_bits:
        pl.semaphore_signal(barrier, inc=1, device_id={"tp": xor(tp, b)},
                            device_id_type=pl.DeviceIdType.MESH)
    for b in dp_bits:
        pl.semaphore_signal(barrier, inc=1, device_id={"dp": xor(dp, b)},
                            device_id_type=pl.DeviceIdType.MESH)

    for step in (2, ndp - 2):
        pl.semaphore_signal(barrier, inc=1, device_id={"dp": lax.rem(dp + step, ndp)},
                            device_id_type=pl.DeviceIdType.MESH)

    w_copies = [pltpu.make_async_copy(wq_ref, wcat.at[:, 0:head], w_sem),
                pltpu.make_async_copy(wkv_ref, wcat.at[:, head:2 * head], w_sem)]
    for copy in w_copies:
        copy.start()

    def block(d):
        return pl.ds(pl.multiple_of(xor(tp, d) * rows, rows), rows)

    cw = width // AG_CHUNKS

    def cols(c, w=cw):
        return slice(c * w, (c + 1) * w)

    for copy in loads[:2]:
        copy.wait()
    square = jnp.zeros((rows, 1), jnp.float32)
    for c in range(AG_CHUNKS):
        v = x_ref[:, cols(c)].astype(jnp.float32)
        square = square + jnp.sum(v * v, axis=1, keepdims=True)
    inv = 1.0 / jnp.sqrt(square * (1.0 / width) + EPS)
    inv_ref[...] = jnp.broadcast_to(inv, inv_ref.shape)

    half = width // 2
    held = AG_CHUNKS // 2

    def turn(c):
        at = lax.rem(c + held * (1 - x), AG_CHUNKS) * cw
        return pl.ds(pl.multiple_of(at, cw), cw)

    def nx(c, d):
        if d & 1:
            part = normed_x.at[block(d ^ 1), cols(c)]
            return remote(part, part, nx_s.at[1], nx_r.at[held], "tp", 1)
        return remote(normed.at[block(d), turn(c)], normed_x.at[block(d), cols(c)],
                      nx_s.at[0], nx_r.at[c], "dp", 1)

    def nx_all(i, k, at):
        part = normed_x.at[0:length // 2, at]
        return remote(part, part, nx_s.at[i], nx_r.at[k], "tp", 1)

    def ag(c, d):
        b = low_bit(d)
        part = normed.at[block(d ^ b), turn(c)]
        return remote(part, part, ag_s.at[d], ag_r.at[c, d // 2 if b > 1 else 0], "tp", b)

    def other_weight():
        return remote(wkv_ref, wcat.at[:, 2 * head:3 * head], wx_s, wx_r, "tp", 1)

    order = sorted(range(1, ntp), key=lambda d: -low_bit(d))
    for c in range(AG_CHUNKS):
        unit = x_ref[:, turn(c)].astype(jnp.float32) * inv
        normed[block(0), turn(c)] = (unit * gain_ref[:, turn(c)]).astype(jnp.bfloat16)
        if c == 0:
            pl.semaphore_wait(barrier, len(tp_bits) + len(dp_bits) + 2)
        for b in reversed(tp_bits):
            ag(c, b).start()
        if c < held:
            nx(c, 0).start()
        if c == 0:
            other_weight().start()
    for copy in loads[2:]:
        copy.wait()
    part = wcat.at[:, 0:2 * head]
    pltpu.make_async_copy(part, part, w_sem).wait()
    other_weight().wait_recv()
    proj = jnp.zeros((length, 3 * head), jnp.float32)

    def forward(c):
        for d in order:
            if low_bit(d) > 1:
                ag(c, d).wait_recv()
                for b in reversed(tp_bits):
                    if b < low_bit(d):
                        ag(c, d | b).start()
                if c < held:
                    nx(c, d).start()

    def arrive(c, proj):
        part = normed.at[0:length // 2, turn(c)]
        remote(part, part, ag_s.at[1], ag_r.at[c, 0], "tp", 1).wait_recv()
        value = normed[:, turn(c)]
        if c >= held:
            normed_t[cols(c - held), 0:length] = value.T
        return proj + dot(value, wcat[turn(c), :], 1, 0)

    def share(i):
        nx_all(0, i, cols(i)).wait_recv()
        for d in range(0, ntp, 2):
            nx(i, d | 1).start()

    seg_s = jnp.broadcast_to(seg_ref[...].astype(jnp.float32), (length, length))
    seg_t = seg_s.T
    t_at = lax.broadcasted_iota(jnp.int32, (length, length), 0)
    s_at = lax.broadcasted_iota(jnp.int32, (length, length), 1)
    allowed = (t_at >= s_at) & (seg_s == seg_t)
    keep[...] = allowed.astype(jnp.float32)

    forward(0)
    for c in range(AG_CHUNKS):
        if c + 1 < AG_CHUNKS:
            forward(c + 1)
        if c == AG_CHUNKS - 1:
            for i in range(held - 1):
                share(i)
        proj = arrive(c, proj)

    blocks = half // BLOCK
    chunks = 2 * blocks
    places = chunks + EARLY
    whole = (qg_ref, kvg_ref)
    half_at = pl.ds(pl.multiple_of(x * half, half), half)

    def local_rows(q, n=1):
        at = q % blocks * BLOCK
        return slice(at, at + n * BLOCK)

    def mine_rows(q, n=1):
        return pl.ds(pl.multiple_of(x * half + q % blocks * BLOCK, BLOCK), n * BLOCK)

    def kind(k):
        return 3 if k < 2 * EARLY else (k - EARLY) // blocks

    def mine(k):
        if kind(k) == 3:
            return term_e.at[k]
        if kind(k) == 2:
            return gsum
        return term.at[kind(k), local_rows(k - EARLY), :]

    def came(k, slot):
        return gchain.at[slot] if kind(k) == 2 else chain.at[k, slot]

    def inward(k):
        return to(mine(k), came(k, is_middle), in_s.at[kind(k)], chain_r.at[is_middle, k], "dp", inner_dp)

    def arrived(k, slot):
        return to(mine(k), came(k, slot), in_s.at[kind(k)], chain_r.at[slot, k], "dp", inner_dp)

    def result_part(k):
        if kind(k) == 3:
            return whole_e.at[k]
        if kind(k) == 2:
            return gg_ref.at[:, half_at]
        return whole[kind(k)].at[mine_rows(k - EARLY), :]

    def outward(k):
        part = result_part(k)
        return to(part, part, down_s.at[kind(k)], chain_r.at[1, k], "dp", outer_dp)

    def final(k):
        part = result_part(k)
        there = seen_e.at[k] if kind(k) == 3 else part
        return remote(part, there, last_s.at[kind(k)], last_r.at[kind(k)], "dp", 1)

    def early_form():
        for h in range(2):
            at = slice(h * half, h * half + EARLY * BLOCK)
            value = dot(normed[:, at], grads[:, :head], 0, 0).astype(jnp.bfloat16)
            for i in range(EARLY):
                term_e[h * EARLY + i] = value[i * BLOCK:(i + 1) * BLOCK, :]

        @pl.when(depth == 0)
        def _():
            for k in range(2 * EARLY):
                inward(k).start()

    def early_end():
        part = whole_e.at[...]
        remote(part, seen_e.at[...], last_s.at[3], last_r.at[3], "dp", 1).wait_recv()
        for h in range(2):
            for i in range(EARLY):
                k = h * EARLY + i
                value = whole_e[k].astype(jnp.float32) + seen_e[k].astype(jnp.float32)
                qg_ref[h * half + i * BLOCK:h * half + (i + 1) * BLOCK, :] = value.astype(jnp.bfloat16)

    def early_weigh():
        value = dot(normed_t[0:EARLY * BLOCK, :], both[:, :head], 1, 0)
        weigh[0:EARLY * BLOCK, :] = value * wcat[mine_rows(0, EARLY), :head].astype(jnp.float32)

    def form(q, n):
        p = q // blocks
        at = slice(p * head, (p + 1) * head)
        local = local_rows(q, n)
        value = dot(normed_t[local, :], both[:, at], 1, 0)
        term[p, local, :] = value.astype(jnp.bfloat16)

        @pl.when(depth == 0)
        def _():
            for i in range(n):
                inward(q + i + EARLY).start()

        value = value * wcat[mine_rows(q, n), at].astype(jnp.float32)
        if p == 0:
            weigh[local, :] = value
        else:
            value = value + weigh[local, :]
            gs[0, :, local] = jnp.sum(value.T, axis=0, keepdims=True)

    def total(k, slot):
        if kind(k) == 2:
            return gsum[...] + gchain[slot]
        return (mine(k)[...].astype(jnp.float32) + chain[k, slot].astype(jnp.float32)).astype(jnp.bfloat16)

    def gather(k):
        @pl.when(depth > 0)
        def _():
            arrived(k, 0).wait_recv()
            mine(k)[...] = total(k, 0)
            inward(k).start()

    def turn_back(k):
        @pl.when(depth == middle)
        def _():
            arrived(k, 1).wait_recv()
            value = total(k, 1)
            result_part(k)[...] = value / gain_ref[:, half_at] if kind(k) == 2 else value
            outward(k).start()
            final(k).start()

    def pass_on(k):
        @pl.when(depth < middle)
        def _():
            outward(k).wait_recv()

            @pl.when(depth > 0)
            def _():
                outward(k).start()

            final(k).start()

    odd = lax.rem(tp, 2) == 1
    cosine, sine = rope_ref[0], rope_ref[1]

    def rope(u):
        return u * cosine + pltpu.roll(u, head // 2, 1) * sine

    def rope_t(u):
        return u * cosine - pltpu.roll(u, head // 2, 1) * sine

    own, other = proj[:, head:2 * head], proj[:, 2 * head:]
    keys = rope(jnp.where(odd, other, own)).astype(jnp.bfloat16)
    values = jnp.where(odd, own, other).astype(jnp.bfloat16)
    query = rope(proj[:, :head]).astype(jnp.bfloat16)
    scale = head ** (-0.5)
    cot = cot_ref[...]
    scores = jnp.where(keep[...] > 0.5, dot(query, keys, 1, 1) * scale, jnp.float32(-1e30))
    top = jnp.max(scores, axis=1, keepdims=True)
    e = jnp.exp(scores - top)
    probs = e / jnp.sum(e, axis=1, keepdims=True)
    prob_grad = dot(cot, values, 1, 1)
    delta = jnp.sum(probs * prob_grad, axis=1, keepdims=True)
    score_grad = (probs * (prob_grad - delta) * scale).astype(jnp.bfloat16)
    grads[:, :head] = rope_t(dot(score_grad, keys, 1, 0)).astype(jnp.bfloat16)

    def gx(p):
        at = slice(p * head, (p + 1) * head)
        return remote(grads.at[:, at], grads_x.at[:, at], gx_s.at[p], gx_r.at[p], "dp", 1)

    gx(0).start()
    early_form()
    share(held - 1)
    key_part = rope_t(dot(score_grad, query, 0, 0))
    value_part = dot(probs.astype(jnp.bfloat16), cot, 0, 0)
    kv_out[...] = jnp.where(odd, key_part, value_part).astype(jnp.bfloat16)
    swap = remote(kv_out, kv_in, kv_s, kv_r, "tp", 1)
    swap.start()
    own_grad = jnp.where(odd, value_part, key_part).astype(jnp.bfloat16).astype(jnp.float32)
    swap.wait_recv()
    grads[:, head:] = (own_grad + kv_in[...].astype(jnp.float32)).astype(jnp.bfloat16)
    gx(1).start()

    rw = width // RS_CHUNKS
    rs_order = sorted(range(1, ntp), key=low_bit)

    def rs(c, d):
        return remote(rs_out.at[d, :, cols(c, rw)], rs_in.at[d, :, cols(c, rw)],
                      rs_s.at[tp_bits.index(low_bit(d))], rs_r.at[c, tp_bits.index(low_bit(d))],
                      "tp", low_bit(d))

    def rs_all(c, at, b):
        n = ntp // (2 * b)
        i = tp_bits.index(b)
        return remote(rs_out.at[0:n, :, at], rs_in.at[0:n, :, at], rs_s.at[i], rs_r.at[c, i], "tp", b)

    def partial(c, d):
        value = tot[block(d), cols(c, rw)]
        for b in tp_bits:
            if d == 0 or b < low_bit(d):
                value = value + rs_in[d | b, :, cols(c, rw)].astype(jnp.float32)
        return value

    def rs_send(c, b):
        for d in rs_order:
            if low_bit(d) == b:
                rs_out[d, :, cols(c, rw)] = partial(c, d).astype(jnp.bfloat16)
                rs(c, d).start()

    def rs_wait(c, b):
        rs_all(c, cols(c, rw), b).wait_recv()

    def back(c):
        tot[:, cols(c, rw)] = dot(grads[...], wcat[cols(c, rw), 0:2 * head], 1, 1)
        rs_send(c, 1)

    def rest(c, b):
        rs_wait(c, b // 2)
        rs_send(c, b)

    scale_back = inv_ref[:, 0:1]

    def exchange(k):
        return remote(gs.at[k], gr.at[k], g_s.at[k], g_r.at[k], "tp", tp_bits[k])

    def add_up(k):
        exchange(k).wait_recv()
        if k + 1 < len(tp_bits):
            gs[k + 1] = gs[k] + gr[k]
            exchange(k + 1).start()
        else:
            gsum[...] = gs[k] + gr[k]

            @pl.when(depth == 0)
            def _():
                inward(places).start()

    inner = [jnp.zeros((rows, 1), jnp.float32)]

    def unit(c):
        return x_ref[:, cols(c, rw)].astype(jnp.float32) * scale_back

    def project(c):
        rs_wait(c, tp_bits[-1])
        scaled = partial(c, 0) * gain_ref[:, cols(c, rw)]
        tot[block(0), cols(c, rw)] = scaled
        inner[0] = inner[0] + jnp.sum(scaled * unit(c), axis=1, keepdims=True)

    def result(c):
        scaled = tot[block(0), cols(c, rw)]
        ig_ref[:, cols(c, rw)] = ((scaled - unit(c) * (inner[0] * (1.0 / width))) * scale_back).astype(jnp.bfloat16)

    work = []

    def later(step, f, *args):
        work.append((step + first, len(work), functools.partial(f, *args)))

    for c in range(FIRST_BACK):
        back(c)
    nx_all(1, held, slice(0, half)).wait_recv()
    for i in range(held):
        normed_t[cols(i), length:2 * length] = normed_x[:, cols(i)].T
    gather(0)
    gx(0).wait_recv()
    q = EARLY
    for i, n in enumerate(QUERY_FORMS):
        form(q, n)
        q = q + n
        if 0 < i < 2 * EARLY:
            gather(i)
    for i in range(len(QUERY_FORMS), 2 * EARLY):
        gather(i)
    first = 2 * EARLY

    for c in range(FIRST_BACK, RS_CHUNKS):
        later(c - FIRST_BACK, back, c)
    later(1, early_weigh)
    later(FORM_AT, lambda: gx(1).wait_recv())
    for i in range(blocks // FORMS):
        at = FORM_AT + FORM_EVERY * i
        later(at, form, blocks + FORMS * i, FORMS)
    later(at, lambda: exchange(0).start())
    for k in range(len(tp_bits)):
        later(at + GAIN_EVERY * (k + 1), add_up, k)
    at = max(GAIN_AT, at + GAIN_EVERY * len(tp_bits) + 1)
    later(at, gather, places)
    later(at + MIDDLE_LAG, turn_back, places)
    later(at + OUTER_LAG, pass_on, places)
    later(EARLY_END, early_end)
    for i, b in enumerate(tp_bits[1:]):
        for c in range(RS_CHUNKS):
            later(REST_AT + i * RS_CHUNKS + c, rest, c, b)
    at = LAST_AT + (len(tp_bits) - 2) * RS_CHUNKS
    for c in range(RS_CHUNKS):
        later(at + 2 * c, project, c)
    for c in range(RS_CHUNKS):
        later(at + 2 * RS_CHUNKS + c, result, c)
    work.sort(key=lambda w: w[:2])
    for step in range(first, places + max(OUTER_LAG, MIDDLE_LAG)):
        if step < places:
            gather(step)
        if 0 <= step - MIDDLE_LAG < places:
            turn_back(step - MIDDLE_LAG)
        if 0 <= step - OUTER_LAG < places:
            pass_on(step - OUTER_LAG)
        while work and work[0][0] <= step:
            work.pop(0)[2]()
    for _, _, f in work:
        f()

    def sent(i):
        if i == 3:
            return term_e, whole_e
        if i == 2:
            return gsum, gg_ref.at[:, half_at]
        start = (1 - i) * EARLY
        return term.at[i, start * BLOCK:half, :], whole[i].at[mine_rows(start, blocks - start), :]

    for i in range(4):
        a, b = sent(i)
        copy = remote(b, b, last_s.at[i], last_r.at[i], "dp", 1)
        copy.wait_send()
        if i < 3:
            copy.wait_recv()
        to(a, a, in_s.at[i], chain_r.at[0, 0], "dp", inner_dp).wait_send()

    @pl.when(depth > 0)
    def _():
        for i in range(4):
            _, b = sent(i)
            to(b, b, down_s.at[i], chain_r.at[1, 0], "dp", outer_dp).wait_send()

    for d in range(1, ntp):
        part = normed.at[block(0), :]
        remote(part, part, ag_s.at[d], ag_r.at[0, 0], "tp", 1).wait_send()
    for i in range(2):
        nx_all(i, held, slice(0, half)).wait_send()
        gx(i).wait_send()
    swap.wait_send()
    other_weight().wait_send()
    for b in tp_bits:
        rs_all(0, slice(0, width), b).wait_send()
        exchange(tp_bits.index(b)).wait_send()


def store(*refs):
    copies = [pltpu.make_async_copy(refs[i], refs[4 + i], refs[8].at[i]) for i in range(4)]
    for copy in copies:
        copy.start()
    for copy in copies:
        copy.wait()


def on_device(ntp, ndp, activations, cotangent, segment_ids, norm_gain, query_weight, key_value_weight):
    rows, width = activations.shape
    length, head = cotangent.shape
    angle = np.arange(length)[:, None] * 500000.0 ** (-np.arange(0, head, 2) / head)[None, :]
    cosine = np.concatenate([np.cos(angle), np.cos(angle)], axis=1).astype(np.float32)
    sine = np.concatenate([-np.sin(angle), np.sin(angle)], axis=1).astype(np.float32)
    chunks = width // BLOCK
    nb = len(bits_of(ntp))
    bf, f32 = jnp.bfloat16, jnp.float32
    vmem = pl.BlockSpec(memory_space=pltpu.VMEM)
    anywhere = pl.BlockSpec(memory_space=pl.ANY)
    hbm = pl.BlockSpec(memory_space=pltpu.HBM)
    dma = pltpu.SemaphoreType.DMA
    outs = pl.pallas_call(
        functools.partial(kernel, ntp, ndp),
        out_shape=[
            pltpu.VMEM((rows, width), bf),
            pltpu.VMEM((width, head), bf),
            pltpu.VMEM((width, head), bf),
            pltpu.VMEM((1, width), f32),
        ],
        in_specs=[hbm] * 7,
        out_specs=[vmem, vmem, vmem, vmem],
        scratch_shapes=[
            pltpu.VMEM((width, 3 * head), bf),
            pltpu.VMEM((length, width), bf),
            pltpu.VMEM((length, width // 2), bf),
            pltpu.VMEM((width // 2, 2 * length), bf),
            pltpu.VMEM((2 * length, 2 * head), bf),
            pltpu.VMEM((length, width), f32),
            pltpu.VMEM((ntp, rows, width), bf),
            pltpu.VMEM((ntp, rows, width), bf),
            pltpu.VMEM((2, width // 2, head), bf),
            pltpu.VMEM((chunks + EARLY, 2, BLOCK, head), bf),
            pltpu.VMEM((2 * EARLY, BLOCK, head), bf),
            pltpu.VMEM((2 * EARLY, BLOCK, head), bf),
            pltpu.VMEM((2 * EARLY, BLOCK, head), bf),
            pltpu.VMEM((width // 2, head), f32),
            pltpu.VMEM((nb, 1, width // 2), f32),
            pltpu.VMEM((nb, 1, width // 2), f32),
            pltpu.VMEM((1, width // 2), f32),
            pltpu.VMEM((2, 1, width // 2), f32),
            pltpu.VMEM((length, head), bf),
            pltpu.VMEM((length, head), bf),
            pltpu.VMEM((rows, 128), f32),
            dma,
            dma((ntp,)),
            dma((AG_CHUNKS, ntp // 2)),
            dma((2,)),
            dma((AG_CHUNKS // 2 + 1,)),
            dma((2,)),
            dma((2,)),
            dma((nb,)),
            dma((RS_CHUNKS, nb)),
            dma((4,)),
            dma((2, chunks + EARLY + 1)),
            dma((4,)),
            dma((4,)),
            dma((4,)),
            dma((nb,)),
            dma((nb,)),
            dma,
            dma,
            dma,
            dma,
            pltpu.VMEM((length, length), f32),
            pltpu.VMEM((rows, width), bf),
            pltpu.VMEM((length, head), bf),
            pltpu.VMEM((1, length), jnp.int32),
            pltpu.VMEM((1, width), f32),
            pltpu.VMEM((2, length, head), f32),
            dma((5,)),
        ],
        compiler_params=pltpu.CompilerParams(
            collective_id=0, has_side_effects=True, vmem_limit_bytes=40 * 1024 * 1024),
    )(*[pltpu.with_memory_space_constraint(v, pltpu.HBM) for v in (
        activations, cotangent, segment_ids.reshape(1, length), norm_gain.reshape(1, width),
        jnp.asarray(np.stack([cosine, sine])), query_weight, key_value_weight)])
    outs = pl.pallas_call(
        store,
        out_shape=[
            jax.ShapeDtypeStruct((rows, width), bf),
            jax.ShapeDtypeStruct((width, head), bf),
            jax.ShapeDtypeStruct((width, head), bf),
            jax.ShapeDtypeStruct((1, width), f32),
        ],
        in_specs=[vmem] * 4,
        out_specs=[hbm] * 4,
        scratch_shapes=[dma((4,))],
    )(*[pltpu.with_memory_space_constraint(v, pltpu.VMEM) for v in outs])
    return (outs[0], outs[1], outs[2], outs[3].reshape(width))


def solution(mesh):
    return jax.shard_map(
        functools.partial(on_device, mesh.shape["tp"], mesh.shape["dp"]),
        mesh=mesh,
        in_specs=(P(("dp", "tp"), None), P("dp", "tp"), P("dp"), P(), P(None, "tp"), P(None, "tp")),
        out_specs=(P(("dp", "tp"), None), P(None, "tp"), P(None, "tp"), P()),
        check_vma=False,
    )
```

```python
import functools

import jax
import jax.numpy as jnp
import numpy as np
from jax import lax
from jax.experimental import pallas as pl
from jax.experimental.pallas import tpu as pltpu
from jax.sharding import PartitionSpec as P

EPS = 1e-05
AG_CHUNKS = 4
BLOCK = 128
OUTER_LAG, MIDDLE_LAG = 10, 4
RS_CHUNKS = 8
EARLY = 2
QUERY_FORMS = (1, 2, 3, 4, 4)
FIRST_BACK, FORM_AT, FORM_EVERY, FORMS, REST_AT, LAST_AT, GAIN_EVERY, GAIN_AT, EARLY_END = 1, 2, 2, 2, 10, 18, 5, 29, 26


def low_bit(d):
    return d & -d


def bits_of(n):
    return [1 << k for k in range(n.bit_length() - 1)]


def bit_at(v, b):
    return lax.rem(lax.div(v, b), 2)


def xor(v, mask):
    out = v
    for b in bits_of(1 << mask.bit_length()):
        if mask & b:
            out = out + b - 2 * b * bit_at(v, b)
    return out


def dot(a, b, ca, cb):
    return lax.dot_general(a, b, (((ca,), (cb,)), ((), ())), preferred_element_type=jnp.float32)


def kernel(ntp, ndp, x_hbm, cot_hbm, seg_hbm, gain_hbm, rope_hbm, wq_ref, wkv_ref,
           ig_ref, qg_ref, kvg_ref, gg_ref,
           wcat, normed, normed_x, normed_t, both, tot, rs_out, rs_in, term, chain, term_e, whole_e, seen_e, weigh, gs, gr, gsum, gchain,
           kv_out, kv_in, inv_ref,
           w_sem, ag_s, ag_r, nx_s, nx_r, gx_s, gx_r, rs_s, rs_r, in_s, chain_r, down_s,
           last_s, last_r, g_s, g_r, kv_s, kv_r, wx_s, wx_r,
           keep, x_ref, cot_ref, seg_ref, gain_ref, rope_ref, load_sem):
    tp, dp = lax.axis_index("tp"), lax.axis_index("dp")
    tp_bits, dp_bits = bits_of(ntp), bits_of(ndp)
    rows, width = x_ref.shape
    length = cot_ref.shape[0]
    grads, grads_x = both.at[0:length, :], both.at[length:2 * length, :]
    head = cot_ref.shape[1]
    x, z, deep = lax.rem(dp, 2), lax.div(dp, 2), ndp // 2
    middle = deep // 2 - 1
    side = lax.div(z, deep // 2)
    depth = z + side * (deep - 1 - 2 * z)
    inner_dp = dp + 2 * (1 - 2 * side)
    outer_dp = dp - 2 * (1 - 2 * side)
    is_middle = lax.div(depth, middle) if middle else 1

    def to(src, dst, s, r, axis, device):
        return pltpu.make_async_remote_copy(
            src_ref=src, dst_ref=dst, send_sem=s, recv_sem=r,
            device_id={axis: device}, device_id_type=pl.DeviceIdType.MESH)

    def remote(src, dst, s, r, axis, b):
        return to(src, dst, s, r, axis, xor(tp if axis == "tp" else dp, b))

    loads = [pltpu.make_async_copy(src, dst, load_sem.at[i]) for i, (src, dst) in enumerate((
        (x_hbm, x_ref), (gain_hbm, gain_ref), (cot_hbm, cot_ref), (seg_hbm, seg_ref),
        (rope_hbm, rope_ref)))]
    for copy in loads:
        copy.start()
    barrier = pltpu.get_barrier_semaphore()
    for b in tp_bits:
        pl.semaphore_signal(barrier, inc=1, device_id={"tp": xor(tp, b)},
                            device_id_type=pl.DeviceIdType.MESH)
    for b in dp_bits:
        pl.semaphore_signal(barrier, inc=1, device_id={"dp": xor(dp, b)},
                            device_id_type=pl.DeviceIdType.MESH)

    for step in (2, ndp - 2):
        pl.semaphore_signal(barrier, inc=1, device_id={"dp": lax.rem(dp + step, ndp)},
                            device_id_type=pl.DeviceIdType.MESH)

    w_copies = [pltpu.make_async_copy(wq_ref, wcat.at[:, 0:head], w_sem),
                pltpu.make_async_copy(wkv_ref, wcat.at[:, head:2 * head], w_sem)]
    for copy in w_copies:
        copy.start()

    def block(d):
        return pl.ds(pl.multiple_of(xor(tp, d) * rows, rows), rows)

    cw = width // AG_CHUNKS

    def cols(c, w=cw):
        return slice(c * w, (c + 1) * w)

    for copy in loads[:2]:
        copy.wait()
    square = jnp.zeros((rows, 1), jnp.float32)
    for c in range(AG_CHUNKS):
        v = x_ref[:, cols(c)].astype(jnp.float32)
        square = square + jnp.sum(v * v, axis=1, keepdims=True)
    inv = 1.0 / jnp.sqrt(square * (1.0 / width) + EPS)
    inv_ref[...] = jnp.broadcast_to(inv, inv_ref.shape)

    half = width // 2
    held = AG_CHUNKS // 2

    def turn(c):
        at = lax.rem(c + held * (1 - x), AG_CHUNKS) * cw
        return pl.ds(pl.multiple_of(at, cw), cw)

    def nx(c, d):
        if d & 1:
            part = normed_x.at[block(d ^ 1), cols(c)]
            return remote(part, part, nx_s.at[1], nx_r.at[held], "tp", 1)
        return remote(normed.at[block(d), turn(c)], normed_x.at[block(d), cols(c)],
                      nx_s.at[0], nx_r.at[c], "dp", 1)

    def nx_all(i, k, at):
        part = normed_x.at[0:length // 2, at]
        return remote(part, part, nx_s.at[i], nx_r.at[k], "tp", 1)

    def ag(c, d):
        b = low_bit(d)
        part = normed.at[block(d ^ b), turn(c)]
        return remote(part, part, ag_s.at[d], ag_r.at[c, d // 2 if b > 1 else 0], "tp", b)

    def other_weight():
        return remote(wkv_ref, wcat.at[:, 2 * head:3 * head], wx_s, wx_r, "tp", 1)

    order = sorted(range(1, ntp), key=lambda d: -low_bit(d))
    for c in range(AG_CHUNKS):
        unit = x_ref[:, turn(c)].astype(jnp.float32) * inv
        normed[block(0), turn(c)] = (unit * gain_ref[:, turn(c)]).astype(jnp.bfloat16)
        if c == 0:
            pl.semaphore_wait(barrier, len(tp_bits) + len(dp_bits) + 2)
        for b in reversed(tp_bits):
            ag(c, b).start()
        if c < held:
            nx(c, 0).start()
        if c == 0:
            other_weight().start()
    for copy in loads[2:]:
        copy.wait()
    part = wcat.at[:, 0:2 * head]
    pltpu.make_async_copy(part, part, w_sem).wait()
    other_weight().wait_recv()
    proj = jnp.zeros((length, 3 * head), jnp.float32)

    def forward(c):
        for d in order:
            if low_bit(d) > 1:
                ag(c, d).wait_recv()
                for b in reversed(tp_bits):
                    if b < low_bit(d):
                        ag(c, d | b).start()
                if c < held:
                    nx(c, d).start()

    def arrive(c, proj):
        part = normed.at[0:length // 2, turn(c)]
        remote(part, part, ag_s.at[1], ag_r.at[c, 0], "tp", 1).wait_recv()
        value = normed[:, turn(c)]
        if c >= held:
            normed_t[cols(c - held), 0:length] = value.T
        return proj + dot(value, wcat[turn(c), :], 1, 0)

    def share(i):
        nx_all(0, i, cols(i)).wait_recv()
        for d in range(0, ntp, 2):
            nx(i, d | 1).start()

    seg_s = jnp.broadcast_to(seg_ref[...].astype(jnp.float32), (length, length))
    seg_t = seg_s.T
    t_at = lax.broadcasted_iota(jnp.int32, (length, length), 0)
    s_at = lax.broadcasted_iota(jnp.int32, (length, length), 1)
    allowed = (t_at >= s_at) & (seg_s == seg_t)
    keep[...] = allowed.astype(jnp.float32)

    forward(0)
    for c in range(AG_CHUNKS):
        if c + 1 < AG_CHUNKS:
            forward(c + 1)
        if c == AG_CHUNKS - 1:
            for i in range(held - 1):
                share(i)
        proj = arrive(c, proj)

    blocks = half // BLOCK
    chunks = 2 * blocks
    places = chunks + EARLY
    whole = (qg_ref, kvg_ref)
    half_at = pl.ds(pl.multiple_of(x * half, half), half)

    def local_rows(q, n=1):
        at = q % blocks * BLOCK
        return slice(at, at + n * BLOCK)

    def mine_rows(q, n=1):
        return pl.ds(pl.multiple_of(x * half + q % blocks * BLOCK, BLOCK), n * BLOCK)

    def kind(k):
        return 3 if k < 2 * EARLY else (k - EARLY) // blocks

    def mine(k):
        if kind(k) == 3:
            return term_e.at[k]
        if kind(k) == 2:
            return gsum
        return term.at[kind(k), local_rows(k - EARLY), :]

    def came(k, slot):
        return gchain.at[slot] if kind(k) == 2 else chain.at[k, slot]

    def inward(k):
        return to(mine(k), came(k, is_middle), in_s.at[kind(k)], chain_r.at[is_middle, k], "dp", inner_dp)

    def arrived(k, slot):
        return to(mine(k), came(k, slot), in_s.at[kind(k)], chain_r.at[slot, k], "dp", inner_dp)

    def result_part(k):
        if kind(k) == 3:
            return whole_e.at[k]
        if kind(k) == 2:
            return gg_ref.at[:, half_at]
        return whole[kind(k)].at[mine_rows(k - EARLY), :]

    def outward(k):
        part = result_part(k)
        return to(part, part, down_s.at[kind(k)], chain_r.at[1, k], "dp", outer_dp)

    def final(k):
        part = result_part(k)
        there = seen_e.at[k] if kind(k) == 3 else part
        return remote(part, there, last_s.at[kind(k)], last_r.at[kind(k)], "dp", 1)

    def early_form():
        for h in range(2):
            at = slice(h * half, h * half + EARLY * BLOCK)
            value = dot(normed[:, at], grads[:, :head], 0, 0).astype(jnp.bfloat16)
            for i in range(EARLY):
                term_e[h * EARLY + i] = value[i * BLOCK:(i + 1) * BLOCK, :]

        @pl.when(depth == 0)
        def _():
            for k in range(2 * EARLY):
                inward(k).start()

    def early_end():
        part = whole_e.at[...]
        remote(part, seen_e.at[...], last_s.at[3], last_r.at[3], "dp", 1).wait_recv()
        for h in range(2):
            for i in range(EARLY):
                k = h * EARLY + i
                value = whole_e[k].astype(jnp.float32) + seen_e[k].astype(jnp.float32)
                qg_ref[h * half + i * BLOCK:h * half + (i + 1) * BLOCK, :] = value.astype(jnp.bfloat16)

    def early_weigh():
        value = dot(normed_t[0:EARLY * BLOCK, :], both[:, :head], 1, 0)
        weigh[0:EARLY * BLOCK, :] = value * wcat[mine_rows(0, EARLY), :head].astype(jnp.float32)

    def form(q, n):
        p = q // blocks
        at = slice(p * head, (p + 1) * head)
        local = local_rows(q, n)
        value = dot(normed_t[local, :], both[:, at], 1, 0)
        term[p, local, :] = value.astype(jnp.bfloat16)

        @pl.when(depth == 0)
        def _():
            for i in range(n):
                inward(q + i + EARLY).start()

        value = value * wcat[mine_rows(q, n), at].astype(jnp.float32)
        if p == 0:
            weigh[local, :] = value
        else:
            value = value + weigh[local, :]
            gs[0, :, local] = jnp.sum(value.T, axis=0, keepdims=True)

    def total(k, slot):
        if kind(k) == 2:
            return gsum[...] + gchain[slot]
        return (mine(k)[...].astype(jnp.float32) + chain[k, slot].astype(jnp.float32)).astype(jnp.bfloat16)

    def gather(k):
        @pl.when(depth > 0)
        def _():
            arrived(k, 0).wait_recv()
            mine(k)[...] = total(k, 0)
            inward(k).start()

    def turn_back(k):
        @pl.when(depth == middle)
        def _():
            arrived(k, 1).wait_recv()
            value = total(k, 1)
            result_part(k)[...] = value / gain_ref[:, half_at] if kind(k) == 2 else value
            outward(k).start()
            final(k).start()

    def pass_on(k):
        @pl.when(depth < middle)
        def _():
            outward(k).wait_recv()

            @pl.when(depth > 0)
            def _():
                outward(k).start()

            final(k).start()

    odd = lax.rem(tp, 2) == 1
    cosine, sine = rope_ref[0], rope_ref[1]

    def rope(u):
        return u * cosine + pltpu.roll(u, head // 2, 1) * sine

    def rope_t(u):
        return u * cosine - pltpu.roll(u, head // 2, 1) * sine

    own, other = proj[:, head:2 * head], proj[:, 2 * head:]
    keys = rope(jnp.where(odd, other, own)).astype(jnp.bfloat16)
    values = jnp.where(odd, own, other).astype(jnp.bfloat16)
    query = rope(proj[:, :head]).astype(jnp.bfloat16)
    scale = head ** (-0.5)
    cot = cot_ref[...]
    scores = jnp.where(keep[...] > 0.5, dot(query, keys, 1, 1) * scale, jnp.float32(-1e30))
    top = jnp.max(scores, axis=1, keepdims=True)
    e = jnp.exp(scores - top)
    probs = e / jnp.sum(e, axis=1, keepdims=True)
    prob_grad = dot(cot, values, 1, 1)
    delta = jnp.sum(probs * prob_grad, axis=1, keepdims=True)
    score_grad = (probs * (prob_grad - delta) * scale).astype(jnp.bfloat16)
    grads[:, :head] = rope_t(dot(score_grad, keys, 1, 0)).astype(jnp.bfloat16)

    def gx(p):
        at = slice(p * head, (p + 1) * head)
        return remote(grads.at[:, at], grads_x.at[:, at], gx_s.at[p], gx_r.at[p], "dp", 1)

    gx(0).start()
    early_form()
    share(held - 1)
    key_part = rope_t(dot(score_grad, query, 0, 0))
    value_part = dot(probs.astype(jnp.bfloat16), cot, 0, 0)
    kv_out[...] = jnp.where(odd, key_part, value_part).astype(jnp.bfloat16)
    swap = remote(kv_out, kv_in, kv_s, kv_r, "tp", 1)
    swap.start()
    own_grad = jnp.where(odd, value_part, key_part).astype(jnp.bfloat16).astype(jnp.float32)
    swap.wait_recv()
    grads[:, head:] = (own_grad + kv_in[...].astype(jnp.float32)).astype(jnp.bfloat16)
    gx(1).start()

    rw = width // RS_CHUNKS
    rs_order = sorted(range(1, ntp), key=low_bit)

    def rs(c, d):
        return remote(rs_out.at[d, :, cols(c, rw)], rs_in.at[d, :, cols(c, rw)],
                      rs_s.at[tp_bits.index(low_bit(d))], rs_r.at[c, tp_bits.index(low_bit(d))],
                      "tp", low_bit(d))

    def rs_all(c, at, b):
        n = ntp // (2 * b)
        i = tp_bits.index(b)
        return remote(rs_out.at[0:n, :, at], rs_in.at[0:n, :, at], rs_s.at[i], rs_r.at[c, i], "tp", b)

    def partial(c, d):
        value = tot[block(d), cols(c, rw)]
        for b in tp_bits:
            if d == 0 or b < low_bit(d):
                value = value + rs_in[d | b, :, cols(c, rw)].astype(jnp.float32)
        return value

    def rs_send(c, b):
        for d in rs_order:
            if low_bit(d) == b:
                rs_out[d, :, cols(c, rw)] = partial(c, d).astype(jnp.bfloat16)
                rs(c, d).start()

    def rs_wait(c, b):
        rs_all(c, cols(c, rw), b).wait_recv()

    def back(c):
        tot[:, cols(c, rw)] = dot(grads[...], wcat[cols(c, rw), 0:2 * head], 1, 1)
        rs_send(c, 1)

    def rest(c, b):
        rs_wait(c, b // 2)
        rs_send(c, b)

    scale_back = inv_ref[:, 0:1]

    def exchange(k):
        return remote(gs.at[k], gr.at[k], g_s.at[k], g_r.at[k], "tp", tp_bits[k])

    def add_up(k):
        exchange(k).wait_recv()
        if k + 1 < len(tp_bits):
            gs[k + 1] = gs[k] + gr[k]
            exchange(k + 1).start()
        else:
            gsum[...] = gs[k] + gr[k]

            @pl.when(depth == 0)
            def _():
                inward(places).start()

    inner = [jnp.zeros((rows, 1), jnp.float32)]

    def unit(c):
        return x_ref[:, cols(c, rw)].astype(jnp.float32) * scale_back

    def project(c):
        rs_wait(c, tp_bits[-1])
        scaled = partial(c, 0) * gain_ref[:, cols(c, rw)]
        tot[block(0), cols(c, rw)] = scaled
        inner[0] = inner[0] + jnp.sum(scaled * unit(c), axis=1, keepdims=True)

    def result(c):
        scaled = tot[block(0), cols(c, rw)]
        ig_ref[:, cols(c, rw)] = ((scaled - unit(c) * (inner[0] * (1.0 / width))) * scale_back).astype(jnp.bfloat16)

    work = []

    def later(step, f, *args):
        work.append((step + first, len(work), functools.partial(f, *args)))

    for c in range(FIRST_BACK):
        back(c)
    nx_all(1, held, slice(0, half)).wait_recv()
    for i in range(held):
        normed_t[cols(i), length:2 * length] = normed_x[:, cols(i)].T
    gather(0)
    gx(0).wait_recv()
    q = EARLY
    for i, n in enumerate(QUERY_FORMS):
        form(q, n)
        q = q + n
        if 0 < i < 2 * EARLY:
            gather(i)
    for i in range(len(QUERY_FORMS), 2 * EARLY):
        gather(i)
    first = 2 * EARLY

    for c in range(FIRST_BACK, RS_CHUNKS):
        later(c - FIRST_BACK, back, c)
    later(1, early_weigh)
    later(FORM_AT, lambda: gx(1).wait_recv())
    for i in range(blocks // FORMS):
        at = FORM_AT + FORM_EVERY * i
        later(at, form, blocks + FORMS * i, FORMS)
    later(at, lambda: exchange(0).start())
    for k in range(len(tp_bits)):
        later(at + GAIN_EVERY * (k + 1), add_up, k)
    at = max(GAIN_AT, at + GAIN_EVERY * len(tp_bits) + 1)
    later(at, gather, places)
    later(at + MIDDLE_LAG, turn_back, places)
    later(at + OUTER_LAG, pass_on, places)
    later(EARLY_END, early_end)
    for i, b in enumerate(tp_bits[1:]):
        for c in range(RS_CHUNKS):
            later(REST_AT + i * RS_CHUNKS + c, rest, c, b)
    at = LAST_AT + (len(tp_bits) - 2) * RS_CHUNKS
    for c in range(RS_CHUNKS):
        later(at + 2 * c, project, c)
    for c in range(RS_CHUNKS):
        later(at + 2 * RS_CHUNKS + c, result, c)
    work.sort(key=lambda w: w[:2])
    for step in range(first, places + max(OUTER_LAG, MIDDLE_LAG)):
        if step < places:
            gather(step)
        if 0 <= step - MIDDLE_LAG < places:
            turn_back(step - MIDDLE_LAG)
        if 0 <= step - OUTER_LAG < places:
            pass_on(step - OUTER_LAG)
        while work and work[0][0] <= step:
            work.pop(0)[2]()
    for _, _, f in work:
        f()

    def sent(i):
        if i == 3:
            return term_e, whole_e
        if i == 2:
            return gsum, gg_ref.at[:, half_at]
        start = (1 - i) * EARLY
        return term.at[i, start * BLOCK:half, :], whole[i].at[mine_rows(start, blocks - start), :]

    for i in range(4):
        a, b = sent(i)
        copy = remote(b, b, last_s.at[i], last_r.at[i], "dp", 1)
        copy.wait_send()
        if i < 3:
            copy.wait_recv()
        to(a, a, in_s.at[i], chain_r.at[0, 0], "dp", inner_dp).wait_send()

    @pl.when(depth > 0)
    def _():
        for i in range(4):
            _, b = sent(i)
            to(b, b, down_s.at[i], chain_r.at[1, 0], "dp", outer_dp).wait_send()

    for d in range(1, ntp):
        part = normed.at[block(0), :]
        remote(part, part, ag_s.at[d], ag_r.at[0, 0], "tp", 1).wait_send()
    for i in range(2):
        nx_all(i, held, slice(0, half)).wait_send()
        gx(i).wait_send()
    swap.wait_send()
    other_weight().wait_send()
    for b in tp_bits:
        rs_all(0, slice(0, width), b).wait_send()
        exchange(tp_bits.index(b)).wait_send()


def store(*refs):
    copies = [pltpu.make_async_copy(refs[i], refs[4 + i], refs[8].at[i]) for i in range(4)]
    for copy in copies:
        copy.start()
    for copy in copies:
        copy.wait()


def on_device(ntp, ndp, activations, cotangent, segment_ids, norm_gain, query_weight, key_value_weight):
    rows, width = activations.shape
    length, head = cotangent.shape
    angle = np.arange(length)[:, None] * 500000.0 ** (-np.arange(0, head, 2) / head)[None, :]
    cosine = np.concatenate([np.cos(angle), np.cos(angle)], axis=1).astype(np.float32)
    sine = np.concatenate([-np.sin(angle), np.sin(angle)], axis=1).astype(np.float32)
    chunks = width // BLOCK
    nb = len(bits_of(ntp))
    bf, f32 = jnp.bfloat16, jnp.float32
    vmem = pl.BlockSpec(memory_space=pltpu.VMEM)
    anywhere = pl.BlockSpec(memory_space=pl.ANY)
    hbm = pl.BlockSpec(memory_space=pltpu.HBM)
    dma = pltpu.SemaphoreType.DMA
    outs = pl.pallas_call(
        functools.partial(kernel, ntp, ndp),
        out_shape=[
            pltpu.VMEM((rows, width), bf),
            pltpu.VMEM((width, head), bf),
            pltpu.VMEM((width, head), bf),
            pltpu.VMEM((1, width), f32),
        ],
        in_specs=[hbm] * 7,
        out_specs=[vmem, vmem, vmem, vmem],
        scratch_shapes=[
            pltpu.VMEM((width, 3 * head), bf),
            pltpu.VMEM((length, width), bf),
            pltpu.VMEM((length, width // 2), bf),
            pltpu.VMEM((width // 2, 2 * length), bf),
            pltpu.VMEM((2 * length, 2 * head), bf),
            pltpu.VMEM((length, width), f32),
            pltpu.VMEM((ntp, rows, width), bf),
            pltpu.VMEM((ntp, rows, width), bf),
            pltpu.VMEM((2, width // 2, head), bf),
            pltpu.VMEM((chunks + EARLY, 2, BLOCK, head), bf),
            pltpu.VMEM((2 * EARLY, BLOCK, head), bf),
            pltpu.VMEM((2 * EARLY, BLOCK, head), bf),
            pltpu.VMEM((2 * EARLY, BLOCK, head), bf),
            pltpu.VMEM((width // 2, head), f32),
            pltpu.VMEM((nb, 1, width // 2), f32),
            pltpu.VMEM((nb, 1, width // 2), f32),
            pltpu.VMEM((1, width // 2), f32),
            pltpu.VMEM((2, 1, width // 2), f32),
            pltpu.VMEM((length, head), bf),
            pltpu.VMEM((length, head), bf),
            pltpu.VMEM((rows, 128), f32),
            dma,
            dma((ntp,)),
            dma((AG_CHUNKS, ntp // 2)),
            dma((2,)),
            dma((AG_CHUNKS // 2 + 1,)),
            dma((2,)),
            dma((2,)),
            dma((nb,)),
            dma((RS_CHUNKS, nb)),
            dma((4,)),
            dma((2, chunks + EARLY + 1)),
            dma((4,)),
            dma((4,)),
            dma((4,)),
            dma((nb,)),
            dma((nb,)),
            dma,
            dma,
            dma,
            dma,
            pltpu.VMEM((length, length), f32),
            pltpu.VMEM((rows, width), bf),
            pltpu.VMEM((length, head), bf),
            pltpu.VMEM((1, length), jnp.int32),
            pltpu.VMEM((1, width), f32),
            pltpu.VMEM((2, length, head), f32),
            dma((5,)),
        ],
        compiler_params=pltpu.CompilerParams(
            collective_id=0, has_side_effects=True, vmem_limit_bytes=40 * 1024 * 1024),
    )(*[pltpu.with_memory_space_constraint(v, pltpu.HBM) for v in (
        activations, cotangent, segment_ids.reshape(1, length), norm_gain.reshape(1, width),
        jnp.asarray(np.stack([cosine, sine])), query_weight, key_value_weight)])
    outs = pl.pallas_call(
        store,
        out_shape=[
            jax.ShapeDtypeStruct((rows, width), bf),
            jax.ShapeDtypeStruct((width, head), bf),
            jax.ShapeDtypeStruct((width, head), bf),
            jax.ShapeDtypeStruct((1, width), f32),
        ],
        in_specs=[vmem] * 4,
        out_specs=[hbm] * 4,
        scratch_shapes=[dma((4,))],
    )(*[pltpu.with_memory_space_constraint(v, pltpu.VMEM) for v in outs])
    return (outs[0], outs[1], outs[2], outs[3].reshape(width))


def solution(mesh):
    return jax.shard_map(
        functools.partial(on_device, mesh.shape["tp"], mesh.shape["dp"]),
        mesh=mesh,
        in_specs=(P(("dp", "tp"), None), P("dp", "tp"), P("dp"), P(), P(None, "tp"), P(None, "tp")),
        out_specs=(P(("dp", "tp"), None), P(None, "tp"), P(None, "tp"), P()),
        check_vma=False,
    )
```
